32 devices in a mesh: lon: 4 (over x, core), lat: 2 (over y), frame: 4 (over z).
Axes of the slice: x: 2, y: 2, z: 4, core: 2. Of those that a mesh axis runs over, the one named last changes fastest.
Arguments:
- features: bfloat16 [4, 128, 64, 256], P('frame', 'lon', 'lat'), may hold values from -6 to 6
- cotangent: bfloat16 [4, 128, 64, 162], P('frame', 'lon', 'lat'), may hold values from -6 to 6
Outputs:
- grads: bfloat16 [4, 128, 64, 256], P('frame', 'lon', 'lat')
The draws below stay inside these ranges and needn't reach their ends.
All inputs are finite; a program needn't handle non-finite values.
Results may differ from the reference program's by a relative error of at most 0.0023.
Values may be sent and summed in bfloat16 or wider, within the bound.
A program may use at most 64 MiB of HBM per device.

```python
import jax
import jax.numpy as jnp
import numpy as np
from jax import lax

CHANNELS = 256
LEVELS = 2
RAD = 4
LON_DEV = 32
LAT_DEV = 32
RIM = 8
FRAMES = 4
NLON = 128
NLAT = 64
N_LON = 4
N_LAT = 2


def levels(rng, shape, shards, least, high):
    def one(dim, blocks):
        draws = jax.random.uniform(jax.random.fold_in(jax.random.fold_in(rng, 6), dim), (blocks,), jnp.float32, least / len(shards), high / len(shards))
        return jnp.repeat(jnp.exp(draws), shape[dim] // blocks).reshape((-1,) + (1,) * (len(shape) - dim - 1))

    loudness = one(*shards[0])
    for cut in shards[1:]:
        loudness = loudness * one(*cut)
    return loudness


def centred(own_key, dims, scale, bound, cuts=(), held_as=jnp.bfloat16):
    entries = scale * jax.random.normal(own_key, dims, jnp.float32)
    if cuts:
        entries = entries * levels(own_key, dims, cuts, -0.22, 0.18)
    return jnp.clip(entries, -bound, bound).astype(held_as)


def setup_inputs(seed: int = 0) -> dict:
    splits = jax.random.split(jax.random.key(seed), 3)
    return {
        "features": centred(splits[0], (FRAMES, NLON, NLAT, CHANNELS), 1.0, 6.0, ((0, 4), (1, 4), (2, 2))),
        "cotangent": centred(splits[1], (FRAMES, NLON, NLAT, LEVELS * (2 * RAD + 1) * (2 * RAD + 1)), 1.0, 6.0, ((0, 4), (1, 4), (2, 2))),
    }


def pooled(extended, factor):
    if factor == 1:
        return extended
    count_x, count_y, channels = extended.shape
    grouped = extended.astype(jnp.float32).reshape(count_x // factor, factor, count_y // factor, factor, channels)
    return (lax.optimization_barrier(jnp.sum(grouped, axis=(1, 3))) / (factor * factor)).astype(jnp.bfloat16)

def query_grad(cot_tile, next_ext):
    tile_cols, tile_rows = (cot_tile.shape[0], cot_tile.shape[1])
    across = 2 * RAD + 1
    stride = 4
    summed = jnp.zeros((tile_cols, tile_rows, next_ext.shape[2]), jnp.float32)
    for pyramid_level in range(LEVELS):
        factor = 2 ** pyramid_level
        anchor = RIM // factor - RAD
        key_rows = tile_rows // factor + 2 * RAD
        key_map = pooled(next_ext, factor)[:, anchor:anchor + key_rows]
        selector = jnp.asarray((np.arange(key_rows)[None, :, None] == (np.arange(tile_rows) // factor)[:, None, None] + np.arange(across)[None, None, :]).astype(np.float32))
        first_chan = pyramid_level * across * across

        def one_block(position):
            start_col = position * stride
            key_block = lax.dynamic_slice_in_dim(key_map, (start_col // factor + anchor).astype(jnp.int32), stride // factor + 2 * RAD, 0)
            window = jnp.stack([jnp.repeat(key_block[shift_col:shift_col + stride // factor], factor, axis=0) for shift_col in range(across)], axis=1)
            window = window.reshape(stride, across * key_rows, window.shape[3]).astype(jnp.float32)
            cot_block = lax.dynamic_slice_in_dim(cot_tile, start_col.astype(jnp.int32), stride, 0)
            portion = cot_block[:, :, first_chan:first_chan + across * across].reshape(stride, tile_rows, across, across).astype(jnp.float32)
            banded = jnp.einsum('xyad,yrd->xyar', portion, selector.astype(jnp.float32))
            banded = banded.reshape(stride, tile_rows, across * key_rows)
            return jnp.einsum('xyk,xkc->xyc', banded, window)
        gradient = lax.map(one_block, jnp.arange(tile_cols // stride, dtype=jnp.int32))
        summed = summed + gradient.reshape(tile_cols, tile_rows, -1)
    return summed * next_ext.shape[2] ** (-0.5)

def key_grad(query_ext, cot_ext):
    tile_cols = query_ext.shape[0] - 2 * RIM
    tile_rows = query_ext.shape[1] - 2 * RIM
    across = 2 * RAD + 1
    summed = jnp.zeros((tile_cols, tile_rows, query_ext.shape[2]), jnp.float32)
    for pyramid_level in range(LEVELS):
        factor = 2 ** pyramid_level
        anchor = RIM - RAD * factor
        row_count = tile_rows + 2 * RAD * factor
        key_cols = tile_cols // factor
        key_rows = tile_rows // factor
        stride = max(1, 4 // factor)
        reach = across * factor
        selector = jnp.asarray((np.arange(key_rows)[:, None, None] == (np.arange(row_count) // factor)[None, :, None] + np.arange(across)[None, None, :] - 2 * RAD).astype(np.float32))
        first_chan = pyramid_level * across * across
        feat_rows = query_ext[:, anchor:anchor + row_count]
        cot_rows = cot_ext[:, anchor:anchor + row_count, first_chan:first_chan + across * across].reshape(cot_ext.shape[0], row_count, across, across)

        def one_block(position):
            start_col = (position * stride * factor + anchor).astype(jnp.int32)
            extent = factor * (stride + 2 * RAD)
            feat_block = lax.dynamic_slice_in_dim(feat_rows, start_col, extent, 0)
            cot_block = lax.dynamic_slice_in_dim(cot_rows, start_col, extent, 0)
            window = jnp.stack([feat_block[shift_col:shift_col + factor * stride:factor] for shift_col in range(reach)], axis=1)
            window = window.reshape(stride, reach * row_count, window.shape[3]).astype(jnp.float32)
            portion = jnp.stack([cot_block[shift_col:shift_col + factor * stride:factor, :, 2 * RAD - shift_col // factor] for shift_col in range(reach)], axis=1).astype(jnp.float32)
            banded = jnp.einsum('ujyd,vyd->uvjy', portion, selector.astype(jnp.float32))
            banded = banded.reshape(stride, key_rows, reach * row_count)
            return jnp.einsum('uvk,ukc->uvc', banded, window)
        gradient = lax.map(one_block, jnp.arange(key_cols // stride, dtype=jnp.int32)).reshape(key_cols, key_rows, -1)
        gradient = jnp.repeat(jnp.repeat(gradient, factor, axis=0), factor, axis=1)
        summed = summed + gradient / (factor * factor)
    return summed * query_ext.shape[2] ** (-0.5)

def extend_global(field):
    wrapped = jnp.concatenate([field[-RIM:], field, field[:RIM]], axis=0)
    return jnp.pad(wrapped, ((0, 0), (RIM, RIM), (0, 0)))

def over_tiles(kernel, extended):

    def one_tile(position):
        lon_pos = position // N_LAT
        lat_pos = position % N_LAT
        pieces = tuple((lax.dynamic_slice(item, (lon_pos * LON_DEV, lat_pos * LAT_DEV, jnp.int32(0)), (LON_DEV + 2 * RIM, LAT_DEV + 2 * RIM, item.shape[2])) for item in extended))
        return kernel(pieces)
    tiles_out = lax.map(one_tile, jnp.arange(N_LON * N_LAT, dtype=jnp.int32))
    tiles_out = tiles_out.reshape(N_LON, N_LAT, LON_DEV, LAT_DEV, -1)
    return tiles_out.transpose(0, 2, 1, 3, 4).reshape(N_LON * LON_DEV, N_LAT * LAT_DEV, -1)

def reference(features, cotangent):
    frame_count = features.shape[0]
    carried = jnp.zeros(features.shape[1:], jnp.float32)
    outputs = []
    for frame_pos in range(frame_count):
        if frame_pos + 1 < frame_count:
            next_ext = extend_global(features[frame_pos + 1])
            query_ext = extend_global(features[frame_pos])
            cot_ext = extend_global(cotangent[frame_pos])
            own_grad = over_tiles(lambda pieces: query_grad(pieces[1][RIM:RIM + LON_DEV, RIM:RIM + LAT_DEV], pieces[0]), (next_ext, cot_ext))
            following = over_tiles(lambda pieces: key_grad(pieces[0], pieces[1]), (query_ext, cot_ext))
        else:
            own_grad = jnp.zeros(features.shape[1:], jnp.float32)
            following = jnp.zeros(features.shape[1:], jnp.float32)
        outputs.append((own_grad + carried).astype(jnp.bfloat16))
        carried = following
    return jnp.stack(outputs, axis=0)
```

```python
import functools

import jax
import jax.numpy as jnp
import ml_dtypes
import numpy as np
from jax import lax
from jax.experimental import pallas as pl
from jax.experimental.pallas import tpu as pltpu
from jax.sharding import PartitionSpec as P

LEVELS = 2
RAD = 4
RIM = 8
ACROSS = 2 * RAD + 1
BLOCK = RIM
HALF = RIM // 2
NEAR = ACROSS + BLOCK - 1
FAR = ACROSS + BLOCK // 2 - 1
MESH = pl.DeviceIdType.MESH


def padded(lanes):
    return -(-lanes // 128) * 128


def spreader(wide):
    near, far = padded(NEAR * wide), padded(FAR * wide)
    out = np.zeros((LEVELS * ACROSS * ACROSS, near + far), np.float32)
    for a in range(ACROSS):
        for b in range(ACROSS):
            out[a * ACROSS + b, a * wide + RAD + b] = 1
            out[ACROSS * ACROSS + a * ACROSS + b, near + a * wide + 2 * b] = 1
    return jnp.asarray(out.astype(ml_dtypes.bfloat16))


def sheared(spread, rows, shifts):
    parts = [
        pltpu.roll(spread[i * rows : (i + 1) * rows], shift, 1, stride=1, stride_axis=0)
        for i, shift in enumerate(shifts)
    ]
    return jnp.concatenate(parts, axis=0).astype(jnp.bfloat16)


def pair_sum(value):
    rows = value.shape[0]
    odd = lax.broadcasted_iota(jnp.int32, value.shape, 0) % 2 == 1
    return value + jnp.where(odd, pltpu.roll(value, 1, 0), pltpu.roll(value, rows - 1, 0))


def kernel(
    sizes,
    feat_ref,
    cot_ref,
    spread_ref,
    out_ref,
    land,
    key_low,
    key_high,
    pack_low,
    pack_high,
    key_ext,
    pool,
    near_acc,
    far_acc,
    band_near,
    band_far,
    send_lon,
    recv_lon,
    send_low,
    send_high,
    recv_low,
    recv_high,
    recv_corner,
    send_up,
    recv_up,
    own_acc,
    sent,
    got,
):
    n_lon, n_lat, n_frame = sizes
    cols, rows, chans = feat_ref.shape
    wide = rows + 2 * RIM
    chunks = cols // BLOCK
    scale = chans ** (-0.5)
    f32, bf16 = jnp.float32, jnp.bfloat16
    lon, lat, frame = lax.axis_index("lon"), lax.axis_index("lat"), lax.axis_index("frame")
    has_down, has_up = frame > 0, frame < n_frame - 1
    has_low, has_high = lat > 0, lat < n_lat - 1
    order = [0] + list(range(chunks - 1, 0, -1))

    def lateral(dx, dy):
        return {"lon": lax.rem(lon + dx + n_lon, n_lon), "lat": lat + dy}

    def reaches(dy):
        return {-1: has_low, 0: None, 1: has_high}[dy]

    def when(cond, act):
        if cond is None:
            act()
        else:
            pl.when(cond)(act)

    count = [0]

    class Message:
        def __init__(self, src, dst, dx, dy):
            self.key, self.dy = count[0], dy
            count[0] += 1
            self.copy = lambda: pltpu.make_async_remote_copy(
                src_ref=src,
                dst_ref=dst,
                send_sem=sent.at[self.key],
                recv_sem=got.at[self.key],
                device_id=lateral(dx, dy),
                device_id_type=MESH,
            )

        def start(self):
            when(reaches(self.dy), lambda: self.copy().start())

        def receive(self):
            when(reaches(-self.dy), lambda: self.copy().wait_recv())

        def finish(self):
            when(reaches(self.dy), lambda: self.copy().wait_send())

    def vertical(src, dst, step):
        key = count[0]
        count[0] += 1
        return pltpu.make_async_remote_copy(
            src_ref=src,
            dst_ref=dst,
            send_sem=sent.at[key],
            recv_sem=got.at[key],
            device_id={"frame": frame + step},
            device_id_type=MESH,
        )

    part = lambda ref, start, size: ref.at[pl.ds(start, size)]
    at = lambda i: pl.ds(i * BLOCK, BLOCK)
    downs = [
        vertical(feat_ref.at[at(i)], part(land, RIM + i * BLOCK, BLOCK), -1) for i in range(chunks)
    ]
    ups = [vertical(send_up.at[at(i)], recv_up.at[at(i)], 1) for i in range(chunks)]
    half = chunks * HALF
    key_lat = [
        [
            Message(part(pack_low, i * HALF, HALF), part(key_high, (i + 1) * HALF, HALF), 0, -1),
            Message(part(pack_high, i * HALF, HALF), part(key_low, (i + 1) * HALF, HALF), 0, 1),
        ]
        for i in range(chunks)
    ]
    key_left = [
        Message(part(land, RIM, RIM), part(land, RIM + cols, RIM), -1, 0),
        Message(part(pack_low, 0, HALF), part(key_high, half + HALF, HALF), -1, -1),
        Message(part(pack_high, 0, HALF), part(key_low, half + HALF, HALF), -1, 1),
    ]
    key_right = [
        Message(part(land, cols, RIM), part(land, 0, RIM), 1, 0),
        Message(part(pack_low, half - HALF, HALF), part(key_high, 0, HALF), 1, -1),
        Message(part(pack_high, half - HALF, HALF), part(key_low, 0, HALF), 1, 1),
    ]
    back_lat = [
        [
            Message(part(send_low, (i + 1) * HALF, HALF), part(recv_high, i * HALF, HALF), 0, -1),
            Message(part(send_high, (i + 1) * HALF, HALF), part(recv_low, i * HALF, HALF), 0, 1),
        ]
        for i in range(chunks)
    ]
    back_left = [
        Message(send_lon.at[0], recv_lon.at[0], -1, 0),
        Message(part(send_low, 0, HALF), recv_corner.at[0], -1, -1),
        Message(part(send_high, 0, HALF), recv_corner.at[1], -1, 1),
    ]
    back_right = [
        Message(send_lon.at[1], recv_lon.at[1], 1, 0),
        Message(part(send_low, half + HALF, HALF), recv_corner.at[2], 1, -1),
        Message(part(send_high, half + HALF, HALF), recv_corner.at[3], 1, 1),
    ]

    barrier = pltpu.get_barrier_semaphore()

    def greet(device):
        pl.semaphore_signal(barrier, inc=1, device_id=device, device_id_type=MESH)

    pl.when(has_down)(lambda: greet({"frame": frame - 1}))
    pl.when(has_up)(lambda: greet({"frame": frame + 1}))
    one = lambda cond: jnp.where(cond, 1, 0)

    @pl.when(has_up)
    def _():
        for dy in (0, -1, 1):
            for dx in (-1, 0, 1):
                if dx or dy:
                    when(reaches(dy), lambda: greet(lateral(dx, dy)))

        @pl.when(~has_low)
        def _():
            key_low[...] = jnp.zeros_like(key_low)
            recv_low[...] = jnp.zeros_like(recv_low)
            recv_corner[1] = jnp.zeros(recv_corner.shape[1:], bf16)
            recv_corner[3] = jnp.zeros(recv_corner.shape[1:], bf16)

        @pl.when(~has_high)
        def _():
            key_high[...] = jnp.zeros_like(key_high)
            recv_high[...] = jnp.zeros_like(recv_high)
            recv_corner[0] = jnp.zeros(recv_corner.shape[1:], bf16)
            recv_corner[2] = jnp.zeros(recv_corner.shape[1:], bf16)

        @pl.loop(0, cols + 2 * RIM)
        def _(pos):
            near_acc[pos] = jnp.zeros((wide, chans), f32)

        @pl.loop(0, cols // 2 + RIM)
        def _(pos):
            far_acc[pos] = jnp.zeros((wide, chans), f32)

    lateral_count = 2 + 3 * (one(has_low) + one(has_high))
    pl.semaphore_wait(barrier, one(has_down) + one(has_up) * (1 + lateral_count))

    @pl.when(has_down)
    def _():
        for i in order:
            downs[i].start()

    @pl.when(has_up)
    def _():
        @pl.loop(0, chunks)
        def _(i):
            cot = cot_ref[at(i)].reshape(BLOCK * rows, cot_ref.shape[2])
            spread = jnp.dot(cot, spread_ref[...], preferred_element_type=f32)
            split = band_near.shape[2]
            near = sheared(spread[:, :split], rows, [j * wide for j in range(BLOCK)])
            far = sheared(spread[:, split:], rows, [j // 2 * wide for j in range(BLOCK)])
            band_near[i] = near
            band_far[i] = far
            feats = feat_ref[at(i)].reshape(BLOCK * rows, chans)
            contract = (((0,), (0,)), ((), ()))
            back = lax.dot_general(near, feats, contract, preferred_element_type=f32)
            back = back[: NEAR * wide].reshape(NEAR, wide, chans)
            near_acc[pl.ds(i * BLOCK + RAD, NEAR)] += back
            back = lax.dot_general(far, feats, contract, preferred_element_type=f32)
            back = back[: FAR * wide].reshape(FAR, wide, chans)
            far_acc[pl.ds(i * (BLOCK // 2), FAR)] += back

        def settle(pos):
            both = pair_sum(far_acc[pos]) * 0.25
            first = (near_acc[2 * pos] + both) * scale
            second = (near_acc[2 * pos + 1] + both) * scale
            low = jnp.concatenate([first[:RIM], second[:RIM]], axis=0)
            high = jnp.concatenate([first[RIM + rows :], second[RIM + rows :]], axis=0)
            send_low[pos] = low.astype(bf16)
            send_high[pos] = high.astype(bf16)
            return first[RIM : RIM + rows], second[RIM : RIM + rows]

        @pl.loop(0, HALF)
        def _(pos):
            for side in range(2):
                first, second = settle(pos + side * (half + HALF))
                send_lon[side, 2 * pos] = first.astype(bf16)
                send_lon[side, 2 * pos + 1] = second.astype(bf16)

        for message in back_left + back_right:
            message.start()

        for i in order[::-1]:

            @pl.loop((i + 1) * HALF, (i + 2) * HALF)
            def _(pos):
                first, second = settle(pos)
                near_acc[2 * pos, RIM : RIM + rows] = first
                near_acc[2 * pos + 1, RIM : RIM + rows] = second

            for message in back_lat[i]:
                message.start()

        def forward(i):
            downs[i].wait_recv()

            @pl.loop(i * HALF, (i + 1) * HALF)
            def _(pos):
                first = land[RIM + 2 * pos].astype(f32)
                second = land[RIM + 2 * pos + 1].astype(f32)
                low = jnp.concatenate([first[:RIM], second[:RIM]], axis=0)
                high = jnp.concatenate([first[rows - RIM :], second[rows - RIM :]], axis=0)
                pack_low[pos] = low.astype(bf16)
                pack_high[pos] = high.astype(bf16)

            if i == 0:
                for message in key_left:
                    message.start()
            if i == chunks - 1:
                for message in key_right:
                    message.start()
            for message in key_lat[i]:
                message.start()

        def rise(i):
            edges = []
            for message in back_lat[i]:
                message.receive()
            if i == 0:
                edges.append((1, 3, 2))
                for message in back_right:
                    message.receive()
            if i == chunks - 1:
                edges.append((0, 1, 0))
                for message in back_left:
                    message.receive()

            @pl.loop(0, HALF)
            def _(pos):
                place = i * HALF + pos
                low, high = recv_low[place].astype(f32), recv_high[place].astype(f32)
                for _, low_corner, high_corner in edges:
                    low = low + recv_corner[low_corner, pos].astype(f32)
                    high = high + recv_corner[high_corner, pos].astype(f32)
                for k in range(2):
                    value = near_acc[RIM + 2 * place + k, RIM : RIM + rows]
                    for side, _, _ in edges:
                        value = value + recv_lon[side, 2 * pos + k].astype(f32)
                    cut = slice(k * RIM, (k + 1) * RIM)
                    value = jnp.concatenate(
                        [
                            value[:RIM] + low[cut],
                            value[RIM : rows - RIM],
                            value[rows - RIM :] + high[cut],
                        ],
                        axis=0,
                    )
                    send_up[2 * place + k] = value.astype(bf16)

            ups[i].start()

        forward(order[0])
        for i in order[::-1]:
            rise(i)
            if i == order[-2]:
                forward(order[1])
        for i in order[2:]:
            forward(i)

        def unfold(begin, end):
            @pl.loop(begin, end)
            def _(pos):
                low, high = key_low[pos].astype(f32), key_high[pos].astype(f32)
                values = []
                for k in range(2):
                    cut = slice(k * RIM, (k + 1) * RIM)
                    value = land[2 * pos + k].astype(f32)
                    value = jnp.concatenate([low[cut], value, high[cut]], axis=0)
                    key_ext[2 * pos + k] = value.astype(bf16)
                    values.append(value)
                pool[pos] = (pair_sum(values[0] + values[1]) * 0.25).astype(bf16)

        for message in key_left + key_right:
            message.receive()
        for i in range(chunks):
            for message in key_lat[i]:
                message.receive()
        unfold(0, half + 2 * HALF)

        @pl.loop(0, chunks)
        def _(i):
            keys = key_ext[pl.ds(i * BLOCK + RAD, NEAR)].reshape(NEAR * wide, chans)
            pooled = pool[pl.ds(i * (BLOCK // 2), FAR)].reshape(FAR * wide, chans)
            total = jnp.dot(band_near[i][:, : NEAR * wide], keys, preferred_element_type=f32)
            total += jnp.dot(band_far[i][:, : FAR * wide], pooled, preferred_element_type=f32)
            own_acc[at(i)] = (total * scale).reshape(BLOCK, rows, chans)

    for i in order[::-1]:

        @pl.when(has_down)
        def _():
            ups[i].wait_recv()

        @pl.when(has_down & has_up)
        def _():
            @pl.loop(i * BLOCK, (i + 1) * BLOCK)
            def _(pos):
                out_ref[pos] = (own_acc[pos] + recv_up[pos].astype(f32)).astype(bf16)

        @pl.when(has_down & ~has_up)
        def _():
            out_ref[at(i)] = recv_up[at(i)]

        @pl.when(~has_down & has_up)
        def _():
            out_ref[at(i)] = own_acc[at(i)].astype(bf16)

    @pl.when(has_down)
    def _():
        for i in order:
            downs[i].wait_send()

    @pl.when(has_up)
    def _():
        for i in order:
            ups[i].wait_send()
        for group in key_lat + back_lat + [key_left, key_right, back_left, back_right]:
            for message in group:
                message.finish()


def body(sizes, features, cotangent):
    _, cols, rows, chans = features.shape
    wide = rows + 2 * RIM
    chunks, half = cols // BLOCK, cols // 2
    near, far = padded(NEAR * wide), padded(FAR * wide)
    vmem = pl.BlockSpec(memory_space=pltpu.VMEM)
    short = lambda *dims: pltpu.VMEM(dims + (chans,), jnp.bfloat16)
    full = lambda *dims: pltpu.VMEM(dims + (chans,), jnp.float32)
    messages = 6 * chunks + 12
    out = pl.pallas_call(
        functools.partial(kernel, sizes),
        out_shape=jax.ShapeDtypeStruct((cols, rows, chans), jnp.bfloat16),
        in_specs=[vmem] * 3,
        out_specs=vmem,
        scratch_shapes=[
            short(cols + 2 * RIM, rows),
            short(half + RIM, 2 * RIM),
            short(half + RIM, 2 * RIM),
            short(half, 2 * RIM),
            short(half, 2 * RIM),
            short(cols + 2 * RIM, wide),
            short(half + RIM, wide),
            full(cols + 2 * RIM, wide),
            full(half + RIM, wide),
            pltpu.VMEM((chunks, BLOCK * rows, near), jnp.bfloat16),
            pltpu.VMEM((chunks, BLOCK * rows, far), jnp.bfloat16),
            short(2, RIM, rows),
            short(2, RIM, rows),
            short(half + RIM, 2 * RIM),
            short(half + RIM, 2 * RIM),
            short(half, 2 * RIM),
            short(half, 2 * RIM),
            short(4, HALF, 2 * RIM),
            short(cols, rows),
            short(cols, rows),
            full(cols, rows),
            pltpu.SemaphoreType.DMA((messages,)),
            pltpu.SemaphoreType.DMA((messages,)),
        ],
        cost_estimate=pl.CostEstimate(flops=10**10, bytes_accessed=4 << 20, transcendentals=0),
        compiler_params=pltpu.CompilerParams(
            collective_id=0, has_side_effects=True, vmem_limit_bytes=44 << 20
        ),
    )(features[0], cotangent[0], spreader(wide))
    return out[None]


def solution(mesh):
    spec = P("frame", "lon", "lat", None)
    sizes = tuple(mesh.shape[axis] for axis in ("lon", "lat", "frame"))
    return jax.shard_map(
        functools.partial(body, sizes), mesh=mesh, in_specs=(spec, spec), out_specs=spec, check_vma=False
    )
```

```python
import functools

import jax
import jax.numpy as jnp
import ml_dtypes
import numpy as np
from jax import lax
from jax.experimental import pallas as pl
from jax.experimental.pallas import tpu as pltpu
from jax.sharding import PartitionSpec as P

LEVELS = 2
RAD = 4
RIM = 8
ACROSS = 2 * RAD + 1
BLOCK = RIM
HALF = RIM // 2
NEAR = ACROSS + BLOCK - 1
FAR = ACROSS + BLOCK // 2 - 1
MESH = pl.DeviceIdType.MESH


def padded(lanes):
    return -(-lanes // 128) * 128


def spreader(wide):
    near, far = padded(NEAR * wide), padded(FAR * wide)
    out = np.zeros((LEVELS * ACROSS * ACROSS, near + far), np.float32)
    for a in range(ACROSS):
        for b in range(ACROSS):
            out[a * ACROSS + b, a * wide + RAD + b] = 1
            out[ACROSS * ACROSS + a * ACROSS + b, near + a * wide + 2 * b] = 1
    return jnp.asarray(out.astype(ml_dtypes.bfloat16))


def sheared(spread, rows, shifts):
    parts = [
        pltpu.roll(spread[i * rows : (i + 1) * rows], shift, 1, stride=1, stride_axis=0)
        for i, shift in enumerate(shifts)
    ]
    return jnp.concatenate(parts, axis=0).astype(jnp.bfloat16)


def pair_sum(value):
    rows = value.shape[0]
    odd = lax.broadcasted_iota(jnp.int32, value.shape, 0) % 2 == 1
    return value + jnp.where(odd, pltpu.roll(value, 1, 0), pltpu.roll(value, rows - 1, 0))


def kernel(
    sizes,
    feat_hbm,
    cot_hbm,
    spread_hbm,
    out_ref,
    feat_ref,
    cot_ref,
    spread_ref,
    own_edge,
    own_mid,
    key_edge,
    key_mid,
    key_rim,
    key_ext,
    pool,
    near_acc,
    far_acc,
    band_near,
    band_far,
    send_lon,
    recv_lon,
    send_rim,
    recv_rim,
    recv_corner,
    send_edge,
    send_mid,
    recv_edge,
    recv_mid,
    own_acc,
    near_by,
    sent,
    got,
):
    n_lon, n_lat, n_frame = sizes
    cols, rows, chans = feat_ref.shape
    wide = rows + 2 * RIM
    chunks, last = cols // BLOCK, cols // BLOCK - 1
    half = cols // 2
    middle = slice(RIM, rows - RIM)
    scale = chans ** (-0.5)
    f32, bf16 = jnp.float32, jnp.bfloat16
    lon, lat, frame = lax.axis_index("lon"), lax.axis_index("lat"), lax.axis_index("frame")
    has_down, has_up = frame > 0, frame < n_frame - 1
    has_low, has_high = lat > 0, lat < n_lat - 1
    inner = list(range(1, last))

    def lateral(dx, dy):
        return {"lon": lax.rem(lon + dx + n_lon, n_lon), "lat": lat + dy}

    def reaches(dy):
        return {-1: has_low, 0: None, 1: has_high}[dy]

    def when(cond, act):
        if cond is None:
            act()
        else:
            pl.when(cond)(act)

    count = [0]

    def fresh():
        count[0] += 1
        return count[0] - 1

    class Message:
        def __init__(self, src, dst, dx, dy):
            self.key, self.dy = fresh(), dy
            self.copy = lambda: pltpu.make_async_remote_copy(
                src_ref=src,
                dst_ref=dst,
                send_sem=sent.at[self.key],
                recv_sem=got.at[self.key],
                device_id=lateral(dx, dy),
                device_id_type=MESH,
            )

        def start(self):
            when(reaches(self.dy), lambda: self.copy().start())

        def receive(self):
            when(reaches(-self.dy), lambda: self.copy().wait_recv())

        def finish(self):
            when(reaches(self.dy), lambda: self.copy().wait_send())

    def vertical(src, dst, step):
        key = fresh()
        return pltpu.make_async_remote_copy(
            src_ref=src,
            dst_ref=dst,
            send_sem=sent.at[key],
            recv_sem=got.at[key],
            device_id={"frame": frame + step},
            device_id_type=MESH,
        )

    def local(src, dst):
        copies.append(pltpu.make_async_copy(src, dst, near_by.at[len(copies)]))
        return copies[-1]

    copies = []
    at = lambda i: pl.ds(i * BLOCK, BLOCK)
    part = lambda ref, start, size: ref.at[pl.ds(start, size)]
    pairs = lambda ref, side, start: ref.at[side, pl.ds(start, HALF)]
    both = lambda ref, start: ref.at[:, pl.ds(start, HALF)]

    spread_in = local(spread_hbm, spread_ref)
    feat_in = [local(feat_hbm.at[at(i)], feat_ref.at[at(i)]) for i in range(chunks)]
    cot_in = [local(cot_hbm.at[at(i)], cot_ref.at[at(i)]) for i in range(chunks)]

    down_edge = [
        vertical(both(own_edge, i * HALF), both(key_edge, (i + 1) * HALF), -1) for i in range(chunks)
    ]
    down_mid = [
        vertical(own_mid.at[at(i)], key_mid.at[at(i + 1)], -1) for i in range(chunks)
    ]
    up_edge = [
        vertical(both(send_edge, i * HALF), both(recv_edge, i * HALF), 1) for i in range(chunks)
    ]
    up_mid = [vertical(send_mid.at[at(i)], recv_mid.at[at(i)], 1) for i in range(chunks)]
    key_lat = [
        [
            Message(pairs(key_edge, side, i * HALF), pairs(key_rim, 1 - side, i * HALF), 0, dy)
            for side, dy in ((0, -1), (1, 1))
        ]
        for i in range(1, chunks + 1)
    ]

    def key_side(dx):
        begin, end = (HALF, half + HALF) if dx < 0 else (half, 0)
        return [
            Message(both(key_edge, begin), both(key_edge, end), dx, 0),
            Message(part(key_mid, 2 * begin, RIM), part(key_mid, 2 * end, RIM), dx, 0),
            Message(pairs(key_edge, 0, begin), pairs(key_rim, 1, end), dx, -1),
            Message(pairs(key_edge, 1, begin), pairs(key_rim, 0, end), dx, 1),
        ]

    key_left, key_right = key_side(-1), key_side(1)
    back_lat = [
        [
            Message(pairs(send_rim, side, (i + 1) * HALF), pairs(recv_rim, 1 - side, i * HALF), 0, dy)
            for side, dy in ((0, -1), (1, 1))
        ]
        for i in range(chunks)
    ]

    def back_side(dx):
        side, begin = (0, 0) if dx < 0 else (1, half + HALF)
        return [
            Message(send_lon.at[side], recv_lon.at[side], dx, 0),
            Message(pairs(send_rim, 0, begin), recv_corner.at[side, 1], dx, -1),
            Message(pairs(send_rim, 1, begin), recv_corner.at[side, 0], dx, 1),
        ]

    back_left, back_right = back_side(-1), back_side(1)

    barrier = pltpu.get_barrier_semaphore()

    def greet(device):
        pl.semaphore_signal(barrier, inc=1, device_id=device, device_id_type=MESH)

    for copy in copies[1 : 1 + chunks]:
        copy.start()
    pl.when(has_down)(lambda: greet({"frame": frame - 1}))
    pl.when(has_up)(lambda: greet({"frame": frame + 1}))
    one = lambda cond: jnp.where(cond, 1, 0)

    @pl.when(has_up)
    def _():
        for dy in (0, -1, 1):
            for dx in (-1, 0, 1):
                if dx or dy:
                    when(reaches(dy), lambda: greet(lateral(dx, dy)))
        spread_in.start()
        for copy in cot_in:
            copy.start()

        for side, present in ((0, has_low), (1, has_high)):

            @pl.when(~present)
            def _():
                key_rim[side] = jnp.zeros(key_rim.shape[1:], bf16)
                recv_rim[side] = jnp.zeros(recv_rim.shape[1:], bf16)
                for k in range(2):
                    recv_corner[k, side] = jnp.zeros(recv_corner.shape[2:], bf16)

        @pl.loop(0, cols + 2 * RIM)
        def _(pos):
            near_acc[pos] = jnp.zeros((wide, chans), f32)

        @pl.loop(0, half + RIM)
        def _(pos):
            far_acc[pos] = jnp.zeros((wide, chans), f32)

    for copy in feat_in:
        copy.wait()

    @pl.when(has_down)
    def _():
        @pl.loop(0, half)
        def _(pos):
            first, second = feat_ref[2 * pos].astype(f32), feat_ref[2 * pos + 1].astype(f32)
            low = jnp.concatenate([first[:RIM], second[:RIM]], axis=0)
            high = jnp.concatenate([first[rows - RIM :], second[rows - RIM :]], axis=0)
            own_edge[0, pos] = low.astype(bf16)
            own_edge[1, pos] = high.astype(bf16)
            own_mid[2 * pos] = first[middle].astype(bf16)
            own_mid[2 * pos + 1] = second[middle].astype(bf16)

    lateral_count = 2 + 3 * (one(has_low) + one(has_high))
    pl.semaphore_wait(barrier, one(has_down) + one(has_up) * (1 + lateral_count))

    @pl.when(has_down)
    def _():
        for i in (0, last):
            down_edge[i].start()
            down_mid[i].start()
        for i in inner:
            down_edge[i].start()
        for i in inner:
            down_mid[i].start()

    @pl.when(has_up)
    def _():
        def back(i):
            cot_in[i].wait()
            cot = cot_ref[at(i)].reshape(BLOCK * rows, cot_ref.shape[2])
            spread = jnp.dot(cot, spread_ref[...], preferred_element_type=f32)
            split = band_near.shape[2]
            near = sheared(spread[:, :split], rows, [j * wide for j in range(BLOCK)])
            far = sheared(spread[:, split:], rows, [j // 2 * wide for j in range(BLOCK)])
            band_near[i] = near
            band_far[i] = far
            feats = feat_ref[at(i)].reshape(BLOCK * rows, chans)
            contract = (((0,), (0,)), ((), ()))
            grad = lax.dot_general(near, feats, contract, preferred_element_type=f32)
            grad = grad[: NEAR * wide].reshape(NEAR, wide, chans)
            near_acc[pl.ds(i * BLOCK + RAD, NEAR)] += grad
            grad = lax.dot_general(far, feats, contract, preferred_element_type=f32)
            grad = grad[: FAR * wide].reshape(FAR, wide, chans)
            far_acc[pl.ds(i * (BLOCK // 2), FAR)] += grad

        def settle(pos):
            coarse = pair_sum(far_acc[pos]) * 0.25
            first = (near_acc[2 * pos] + coarse) * scale
            second = (near_acc[2 * pos + 1] + coarse) * scale
            for side, begin in ((0, 0), (1, RIM + rows)):
                cut = slice(begin, begin + RIM)
                send_rim[side, pos] = jnp.concatenate([first[cut], second[cut]], axis=0).astype(bf16)
            return first[RIM : RIM + rows], second[RIM : RIM + rows]

        def settle_side(side):
            @pl.loop(0, HALF)
            def _(pos):
                first, second = settle(pos + side * (half + HALF))
                send_lon[side, 2 * pos] = first.astype(bf16)
                send_lon[side, 2 * pos + 1] = second.astype(bf16)

            for message in (back_left, back_right)[side]:
                message.start()

        def settle_inner(i):
            @pl.loop(0, HALF)
            def _(pos):
                place = i * HALF + pos
                for k, value in enumerate(settle(place + HALF)):
                    near_acc[RIM + 2 * place + k, RIM : RIM + rows] = value
                    if 0 < i < last:
                        send_mid[2 * place + k] = value[middle].astype(bf16)

            for message in back_lat[i]:
                message.start()
            if 0 < i < last:
                up_mid[i].start()

        def forward_edge(i):
            down_edge[i].wait_recv()
            for message in key_lat[i]:
                message.start()
            if i in (0, last):
                down_mid[i].wait_recv()
                for message in key_left if i == 0 else key_right:
                    message.start()

        def rise_edge(i):
            for message in back_lat[i]:
                message.receive()

            @pl.loop(i * HALF, (i + 1) * HALF)
            def _(place):
                for side, begin in ((0, RIM), (1, rows)):
                    value = recv_rim[side, place].astype(f32)
                    own = [
                        near_acc[RIM + 2 * place + k, begin : begin + RIM] for k in range(2)
                    ]
                    value = value + jnp.concatenate(own, axis=0)
                    if i in (0, last):
                        value = value + recv_corner[int(i == 0), side, place - i * HALF].astype(f32)
                    send_edge[side, place] = value.astype(bf16)

            up_edge[i].start()

        def rise_side(i):
            side = int(i == 0)
            for message in (back_left, back_right)[side]:
                message.receive()

            @pl.loop(0, BLOCK)
            def _(pos):
                place = RIM + i * BLOCK + pos
                rim = recv_lon[side, pos].astype(f32)
                value = near_acc[place, RIM : RIM + rows] + rim
                near_acc[place, RIM : RIM + rows] = value
                send_mid[i * BLOCK + pos] = value[middle].astype(bf16)

            up_mid[i].start()

        spread_in.wait()
        for i in range(chunks):
            back(i)
            if i == 0:
                settle_side(0)
            elif i > 1:
                settle_inner(i - 1)
        settle_side(1)
        settle_inner(0)
        settle_inner(last)
        forward_edge(0)
        for i in inner:
            rise_edge(i)
        forward_edge(last)
        for i in (0, last):
            rise_side(i)
            rise_edge(i)
        for i in inner:
            forward_edge(i)

        def unfold(i):
            @pl.loop(i * HALF, (i + 1) * HALF)
            def _(pos):
                rims = [key_rim[side, pos].astype(f32) for side in range(2)]
                edges = [key_edge[side, pos].astype(f32) for side in range(2)]
                values = []
                for k in range(2):
                    cut = slice(k * RIM, (k + 1) * RIM)
                    mid = key_mid[2 * pos + k].astype(f32)
                    value = [rims[0][cut], edges[0][cut], mid, edges[1][cut], rims[1][cut]]
                    value = jnp.concatenate(value, axis=0)
                    key_ext[2 * pos + k] = value.astype(bf16)
                    values.append(value)
                pool[pos] = (pair_sum(values[0] + values[1]) * 0.25).astype(bf16)

        def own(i):
            keys = key_ext[pl.ds(i * BLOCK + RAD, NEAR)].reshape(NEAR * wide, chans)
            pooled = pool[pl.ds(i * (BLOCK // 2), FAR)].reshape(FAR * wide, chans)
            total = jnp.dot(band_near[i, :, : NEAR * wide], keys, preferred_element_type=f32)
            total += jnp.dot(band_far[i, :, : FAR * wide], pooled, preferred_element_type=f32)
            own_acc[at(i)] = (total * scale).reshape(BLOCK, rows, chans)

        for message in key_left + key_right + key_lat[0] + key_lat[last]:
            message.receive()
        for i in (0, 1, last + 1, last + 2):
            unfold(i)
        for i in inner:
            for message in key_lat[i]:
                message.receive()
            down_mid[i].wait_recv()
            unfold(i + 1)
            own(i - 1)
        for i in range(inner[-1], chunks):
            own(i)

    for i in inner + [0, last]:

        @pl.when(has_down)
        def _():
            up_mid[i].wait_recv()
            up_edge[i].wait_recv()

        def carried(place):
            edges = [recv_edge[side, place].astype(f32) for side in range(2)]
            for k in range(2):
                cut = slice(k * RIM, (k + 1) * RIM)
                mid = recv_mid[2 * place + k].astype(f32)
                yield 2 * place + k, jnp.concatenate([edges[0][cut], mid, edges[1][cut]], axis=0)

        @pl.when(has_down & has_up)
        def _():
            @pl.loop(i * HALF, (i + 1) * HALF)
            def _(place):
                for pos, value in carried(place):
                    out_ref[pos] = (own_acc[pos] + value).astype(bf16)

        @pl.when(has_down & ~has_up)
        def _():
            @pl.loop(i * HALF, (i + 1) * HALF)
            def _(place):
                for pos, value in carried(place):
                    out_ref[pos] = value.astype(bf16)

        @pl.when(~has_down & has_up)
        def _():
            out_ref[at(i)] = own_acc[at(i)].astype(bf16)

    @pl.when(has_down)
    def _():
        for copy in down_edge + down_mid:
            copy.wait_send()

    @pl.when(has_up)
    def _():
        for copy in up_edge + up_mid:
            copy.wait_send()
        for group in key_lat + back_lat + [key_left, key_right, back_left, back_right]:
            for message in group:
                message.finish()


def body(sizes, features, cotangent):
    _, cols, rows, chans = features.shape
    wide = rows + 2 * RIM
    chunks, half = cols // BLOCK, cols // 2
    near, far = padded(NEAR * wide), padded(FAR * wide)
    spread = spreader(wide)
    vmem, hbm = (pl.BlockSpec(memory_space=space) for space in (pltpu.VMEM, pltpu.HBM))
    short = lambda *dims: pltpu.VMEM(dims + (chans,), jnp.bfloat16)
    full = lambda *dims: pltpu.VMEM(dims + (chans,), jnp.float32)
    messages = 8 * chunks + 14
    out = pl.pallas_call(
        functools.partial(kernel, sizes),
        out_shape=jax.ShapeDtypeStruct((cols, rows, chans), jnp.bfloat16),
        in_specs=[hbm] * 3,
        out_specs=vmem,
        scratch_shapes=[
            short(cols, rows),
            pltpu.VMEM((cols, rows, cotangent.shape[3]), jnp.bfloat16),
            pltpu.VMEM(spread.shape, jnp.bfloat16),
            short(2, half, 2 * RIM),
            short(cols, rows - 2 * RIM),
            short(2, half + RIM, 2 * RIM),
            short(cols + 2 * RIM, rows - 2 * RIM),
            short(2, half + RIM, 2 * RIM),
            short(cols + 2 * RIM, wide),
            short(half + RIM, wide),
            full(cols + 2 * RIM, wide),
            full(half + RIM, wide),
            pltpu.VMEM((chunks, BLOCK * rows, near), jnp.bfloat16),
            pltpu.VMEM((chunks, BLOCK * rows, far), jnp.bfloat16),
            short(2, RIM, rows),
            short(2, RIM, rows),
            short(2, half + RIM, 2 * RIM),
            short(2, half, 2 * RIM),
            short(2, 2, HALF, 2 * RIM),
            short(2, half, 2 * RIM),
            short(cols, rows - 2 * RIM),
            short(2, half, 2 * RIM),
            short(cols, rows - 2 * RIM),
            full(cols, rows),
            pltpu.SemaphoreType.DMA((1 + 2 * chunks,)),
            pltpu.SemaphoreType.DMA((messages,)),
            pltpu.SemaphoreType.DMA((messages,)),
        ],
        cost_estimate=pl.CostEstimate(flops=10**10, bytes_accessed=4 << 20, transcendentals=0),
        compiler_params=pltpu.CompilerParams(
            collective_id=0, has_side_effects=True, vmem_limit_bytes=56 << 20
        ),
    )(features[0], cotangent[0], spread)
    return out[None]


def solution(mesh):
    spec = P("frame", "lon", "lat", None)
    sizes = tuple(mesh.shape[axis] for axis in ("lon", "lat", "frame"))
    return jax.shard_map(
        functools.partial(body, sizes), mesh=mesh, in_specs=(spec, spec), out_specs=spec, check_vma=False
    )
```

```python
import functools

import jax
import jax.numpy as jnp
from jax import lax
from jax.experimental import pallas as pl
from jax.experimental.pallas import tpu as pltpu
from jax.sharding import PartitionSpec as P

LEVELS = 2
RAD = 4
RIM = 8
ACROSS = 2 * RAD + 1
BLOCK = RIM
HALF = RIM // 2
NEAR = ACROSS + BLOCK - 1
FAR = ACROSS + BLOCK // 2 - 1
MESH = pl.DeviceIdType.MESH


def padded(lanes):
    return -(-lanes // 128) * 128


def spreader(wide):
    near, far = padded(NEAR * wide), padded(FAR * wide)
    shape = (LEVELS * ACROSS * ACROSS, near + far)
    row = lax.broadcasted_iota(jnp.int32, (shape[0], 1), 0)
    fine = row < ACROSS * ACROSS
    row = jnp.where(fine, row, row - ACROSS * ACROSS)
    a = sum((row >= k * ACROSS).astype(jnp.int32) for k in range(1, ACROSS))
    b = row - a * ACROSS
    place = a * wide + jnp.where(fine, RAD + b, near + 2 * b)
    lane = lax.broadcasted_iota(jnp.int32, shape, 1)
    return jnp.where(lane == place, 1.0, 0.0).astype(jnp.bfloat16)


def sheared(spread, rows, shifts):
    parts = [
        pltpu.roll(spread[i * rows : (i + 1) * rows], shift, 1, stride=1, stride_axis=0)
        for i, shift in enumerate(shifts)
    ]
    return jnp.concatenate(parts, axis=0).astype(jnp.bfloat16)


def pair_sum(value):
    rows = value.shape[0]
    odd = lax.broadcasted_iota(jnp.int32, value.shape, 0) % 2 == 1
    return value + jnp.where(odd, pltpu.roll(value, 1, 0), pltpu.roll(value, rows - 1, 0))


def kernel(
    sizes,
    feat_hbm,
    cot_hbm,
    out_ref,
    feat_ref,
    cot_ref,
    spread_ref,
    own_edge,
    own_mid,
    key_edge,
    key_rim,
    key_ext,
    pool,
    near_acc,
    far_acc,
    band_near,
    band_far,
    send_lon,
    recv_lon,
    send_rim,
    recv_rim,
    recv_corner,
    send_edge,
    send_mid,
    recv_edge,
    recv_mid,
    own_acc,
    near_by,
    sent,
    got,
):
    n_lon, n_lat, n_frame = sizes
    cols, rows, chans = feat_ref.shape
    wide = rows + 2 * RIM
    chunks, last = cols // BLOCK, cols // BLOCK - 1
    half = cols // 2
    middle = slice(RIM, rows - RIM)
    scale = chans ** (-0.5)
    f32, bf16 = jnp.float32, jnp.bfloat16
    lon, lat, frame = lax.axis_index("lon"), lax.axis_index("lat"), lax.axis_index("frame")
    has_down, has_up = frame > 0, frame < n_frame - 1
    has_low, has_high = lat > 0, lat < n_lat - 1
    inner = list(range(1, last))

    def lateral(dx, dy):
        return {"lon": lax.rem(lon + dx + n_lon, n_lon), "lat": lat + dy}

    def reaches(dy):
        return {-1: has_low, 0: None, 1: has_high}[dy]

    def when(cond, act):
        if cond is None:
            act()
        else:
            pl.when(cond)(act)

    count = [0]

    def fresh():
        count[0] += 1
        return count[0] - 1

    class Message:
        def __init__(self, src, dst, dx, dy):
            self.key, self.dy = fresh(), dy
            self.copy = lambda: pltpu.make_async_remote_copy(
                src_ref=src,
                dst_ref=dst,
                send_sem=sent.at[self.key],
                recv_sem=got.at[self.key],
                device_id=lateral(dx, dy),
                device_id_type=MESH,
            )

        def start(self):
            when(reaches(self.dy), lambda: self.copy().start())

        def receive(self):
            when(reaches(-self.dy), lambda: self.copy().wait_recv())

        def finish(self):
            when(reaches(self.dy), lambda: self.copy().wait_send())

    def vertical(src, dst, step):
        key = fresh()
        return pltpu.make_async_remote_copy(
            src_ref=src,
            dst_ref=dst,
            send_sem=sent.at[key],
            recv_sem=got.at[key],
            device_id={"frame": frame + step},
            device_id_type=MESH,
        )

    def local(src, dst):
        copies.append(pltpu.make_async_copy(src, dst, near_by.at[len(copies)]))
        return copies[-1]

    copies = []
    at = lambda i: pl.ds(i * BLOCK, BLOCK)
    part = lambda ref, start, size: ref.at[pl.ds(start, size)]
    pairs = lambda ref, side, start: ref.at[side, pl.ds(start, HALF)]
    mids = lambda i: key_ext.at[at(i), pl.ds(2 * RIM, rows - 2 * RIM)]
    both = lambda ref, start: ref.at[:, pl.ds(start, HALF)]

    feat_in = [local(feat_hbm.at[at(i)], feat_ref.at[at(i)]) for i in range(chunks)]
    cot_in = [local(cot_hbm.at[at(i)], cot_ref.at[at(i)]) for i in range(chunks)]

    down_edge = [
        vertical(both(own_edge, i * HALF), both(key_edge, (i + 1) * HALF), -1) for i in range(chunks)
    ]
    down_mid = [
        vertical(own_mid.at[at(i)], mids(i + 1), -1) for i in range(chunks)
    ]
    up_edge = [
        vertical(both(send_edge, i * HALF), both(recv_edge, i * HALF), 1) for i in range(chunks)
    ]
    up_mid = [vertical(send_mid.at[at(i)], recv_mid.at[at(i)], 1) for i in range(chunks)]
    key_lat = [
        [
            Message(pairs(key_edge, side, i * HALF), pairs(key_rim, 1 - side, i * HALF), 0, dy)
            for side, dy in ((0, -1), (1, 1))
        ]
        for i in range(1, chunks + 1)
    ]

    def key_side(dx):
        begin, end = (HALF, half + HALF) if dx < 0 else (half, 0)
        return [
            Message(mids(2 * begin // BLOCK), mids(2 * end // BLOCK), dx, 0),
            Message(both(key_edge, begin), both(key_edge, end), dx, 0),
            Message(pairs(key_edge, 0, begin), pairs(key_rim, 1, end), dx, -1),
            Message(pairs(key_edge, 1, begin), pairs(key_rim, 0, end), dx, 1),
        ]

    key_left, key_right = key_side(-1), key_side(1)
    back_lat = [
        [
            Message(pairs(send_rim, side, (i + 1) * HALF), pairs(recv_rim, 1 - side, i * HALF), 0, dy)
            for side, dy in ((0, -1), (1, 1))
        ]
        for i in range(chunks)
    ]

    def back_side(dx):
        side, begin = (0, 0) if dx < 0 else (1, half + HALF)
        return [
            Message(send_lon.at[side], recv_lon.at[side], dx, 0),
            Message(pairs(send_rim, 0, begin), recv_corner.at[side, 1], dx, -1),
            Message(pairs(send_rim, 1, begin), recv_corner.at[side, 0], dx, 1),
        ]

    back_left, back_right = back_side(-1), back_side(1)

    barrier = pltpu.get_barrier_semaphore()

    def greet(device):
        pl.semaphore_signal(barrier, inc=1, device_id=device, device_id_type=MESH)

    for copy in feat_in:
        copy.start()
    pl.when(has_down)(lambda: greet({"frame": frame - 1}))
    pl.when(has_up)(lambda: greet({"frame": frame + 1}))
    one = lambda cond: jnp.where(cond, 1, 0)

    @pl.when(has_up)
    def _():
        for dy in (0, -1, 1):
            for dx in (-1, 0, 1):
                if dx or dy:
                    when(reaches(dy), lambda: greet(lateral(dx, dy)))
        for copy in cot_in:
            copy.start()

        for side, present in ((0, has_low), (1, has_high)):

            @pl.when(~present)
            def _():
                key_rim[side] = jnp.zeros(key_rim.shape[1:], bf16)
                recv_rim[side] = jnp.zeros(recv_rim.shape[1:], bf16)
                for k in range(2):
                    recv_corner[k, side] = jnp.zeros(recv_corner.shape[2:], bf16)

        spread_ref[...] = spreader(wide)

        for begin in (0, cols + 2 * RIM - RAD):
            near_acc[pl.ds(begin, RAD)] = jnp.zeros((RAD, wide, chans), f32)

    for copy in feat_in:
        copy.wait()

    @pl.when(has_down)
    def _():
        @pl.loop(0, half)
        def _(pos):
            first, second = feat_ref[2 * pos].astype(f32), feat_ref[2 * pos + 1].astype(f32)
            low = jnp.concatenate([first[:RIM], second[:RIM]], axis=0)
            high = jnp.concatenate([first[rows - RIM :], second[rows - RIM :]], axis=0)
            own_edge[0, pos] = low.astype(bf16)
            own_edge[1, pos] = high.astype(bf16)
            own_mid[2 * pos] = first[middle].astype(bf16)
            own_mid[2 * pos + 1] = second[middle].astype(bf16)

    lateral_count = 2 + 3 * (one(has_low) + one(has_high))
    pl.semaphore_wait(barrier, one(has_down) + one(has_up) * (1 + lateral_count))

    @pl.when(has_down)
    def _():
        for i in (0, last):
            down_edge[i].start()
            down_mid[i].start()
        for i in inner:
            down_edge[i].start()
        for i in inner:
            down_mid[i].start()

    @pl.when(has_up)
    def _():
        def add(ref, start, value, held):
            if held:
                ref[pl.ds(start, held)] += value[:held]
            ref[pl.ds(start + held, value.shape[0] - held)] = value[held:]

        def back(i):
            cot_in[i].wait()
            cot = cot_ref[at(i)].reshape(BLOCK * rows, cot_ref.shape[2])
            spread = jnp.dot(cot, spread_ref[...], preferred_element_type=f32)
            split = band_near.shape[2]
            near = sheared(spread[:, :split], rows, [j * wide for j in range(BLOCK)])
            far = sheared(spread[:, split:], rows, [j // 2 * wide for j in range(BLOCK)])
            band_near[i] = near
            band_far[i] = far
            feats = feat_ref[at(i)].reshape(BLOCK * rows, chans)
            contract = (((0,), (0,)), ((), ()))
            grad = lax.dot_general(near, feats, contract, preferred_element_type=f32)
            grad = grad[: NEAR * wide].reshape(NEAR, wide, chans)
            add(near_acc, i * BLOCK + RAD, grad, i and NEAR - BLOCK)
            grad = lax.dot_general(far, feats, contract, preferred_element_type=f32)
            grad = grad[: FAR * wide].reshape(FAR, wide, chans)
            add(far_acc, i * (BLOCK // 2), grad, i and FAR - BLOCK // 2)

        def settle(pos):
            coarse = pair_sum(far_acc[pos]) * 0.25
            first = (near_acc[2 * pos] + coarse) * scale
            second = (near_acc[2 * pos + 1] + coarse) * scale
            for side, begin in ((0, 0), (1, RIM + rows)):
                cut = slice(begin, begin + RIM)
                send_rim[side, pos] = jnp.concatenate([first[cut], second[cut]], axis=0).astype(bf16)
            return first[RIM : RIM + rows], second[RIM : RIM + rows]

        def settle_side(side):
            @pl.loop(0, HALF)
            def _(pos):
                first, second = settle(pos + side * (half + HALF))
                send_lon[side, 2 * pos] = first.astype(bf16)
                send_lon[side, 2 * pos + 1] = second.astype(bf16)

            for message in (back_left, back_right)[side]:
                message.start()

        def settle_inner(i):
            @pl.loop(0, HALF)
            def _(pos):
                place = i * HALF + pos
                for k, value in enumerate(settle(place + HALF)):
                    near_acc[RIM + 2 * place + k, RIM : RIM + rows] = value
                    if 0 < i < last:
                        send_mid[2 * place + k] = value[middle].astype(bf16)

            for message in back_lat[i]:
                message.start()
            if 0 < i < last:
                up_mid[i].start()

        def forward_edge(i):
            down_edge[i].wait_recv()
            for message in key_lat[i]:
                message.start()
            if i in (0, last):
                for message in (key_left if i == 0 else key_right)[1:]:
                    message.start()

        def forward_mid(i):
            down_mid[i].wait_recv()
            (key_left if i == 0 else key_right)[0].start()

        def rise_edge(i):
            for message in back_lat[i]:
                message.receive()

            @pl.loop(i * HALF, (i + 1) * HALF)
            def _(place):
                for side, begin in ((0, RIM), (1, rows)):
                    value = recv_rim[side, place].astype(f32)
                    own = [
                        near_acc[RIM + 2 * place + k, begin : begin + RIM] for k in range(2)
                    ]
                    value = value + jnp.concatenate(own, axis=0)
                    if i in (0, last):
                        value = value + recv_corner[int(i == 0), side, place - i * HALF].astype(f32)
                    send_edge[side, place] = value.astype(bf16)

            up_edge[i].start()

        def rise_side(i):
            side = int(i == 0)
            for message in (back_left, back_right)[side]:
                message.receive()

            @pl.loop(0, BLOCK)
            def _(pos):
                place = RIM + i * BLOCK + pos
                rim = recv_lon[side, pos].astype(f32)
                value = near_acc[place, RIM : RIM + rows] + rim
                near_acc[place, RIM : RIM + rows] = value
                send_mid[i * BLOCK + pos] = value[middle].astype(bf16)

            up_mid[i].start()

        for i in range(chunks):
            back(i)
            if i == 0:
                settle_side(0)
            elif i > 1:
                settle_inner(i - 1)
        settle_side(1)
        settle_inner(0)
        settle_inner(last)
        forward_edge(0)
        rise_edge(inner[0])
        forward_mid(0)
        for i in inner[1:]:
            rise_edge(i)
        forward_edge(last)
        rise_side(last)
        rise_edge(last)
        forward_mid(last)
        rise_side(0)
        rise_edge(0)
        for i in inner:
            forward_edge(i)

        def unfold_edge(i):
            @pl.loop(i * HALF, (i + 1) * HALF)
            def _(pos):
                for side, begin in ((0, 0), (1, rows)):
                    pieces = [ref[side, pos].astype(f32) for ref in (key_rim, key_edge)[:: 1 - 2 * side]]
                    values = []
                    for k in range(2):
                        cut = slice(k * RIM, (k + 1) * RIM)
                        values.append(jnp.concatenate([piece[cut] for piece in pieces], axis=0))
                        key_ext[2 * pos + k, begin : begin + 2 * RIM] = values[k].astype(bf16)
                    pool[pos, begin : begin + 2 * RIM] = pooled(values)

        def unfold_mid(i):
            for pos in range(i * HALF, (i + 1) * HALF):
                values = [key_ext[2 * pos + k, 2 * RIM : rows].astype(f32) for k in range(2)]
                pool[pos, 2 * RIM : rows] = pooled(values)

        def pooled(values):
            return (pair_sum(values[0] + values[1]) * 0.25).astype(bf16)

        def own(i):
            keys = key_ext[pl.ds(i * BLOCK + RAD, NEAR)].reshape(NEAR * wide, chans)
            coarse = pool[pl.ds(i * (BLOCK // 2), FAR)].reshape(FAR * wide, chans)
            total = jnp.dot(band_near[i, :, : NEAR * wide], keys, preferred_element_type=f32)
            total += jnp.dot(band_far[i, :, : FAR * wide], coarse, preferred_element_type=f32)
            total = (total * scale).reshape(BLOCK, rows, chans)
            own_acc[at(i)] = total
            out_ref[at(i)] = total.astype(bf16)

        for message in key_left + key_right + key_lat[0] + key_lat[last]:
            message.receive()
        for i in (0, 1, last + 1, last + 2):
            unfold_edge(i)
            unfold_mid(i)
        for i in inner:
            for message in key_lat[i]:
                message.receive()
            unfold_edge(i + 1)
            if i == inner[-1]:
                for group in key_lat + back_lat + [key_left, key_right, back_left, back_right]:
                    for message in group:
                        message.finish()

                @pl.when(has_down)
                def _():
                    for copy in down_edge + down_mid:
                        copy.wait_send()

            down_mid[i].wait_recv()
            unfold_mid(i + 1)
            own(i - 1)
        for i in range(inner[-1], chunks):
            own(i)

    for i in inner + [last, 0]:

        @pl.when(has_down)
        def _():
            up_mid[i].wait_recv()
            up_edge[i].wait_recv()

        def carried(place):
            edges = [recv_edge[side, place].astype(f32) for side in range(2)]
            for k in range(2):
                cut = slice(k * RIM, (k + 1) * RIM)
                mid = recv_mid[2 * place + k].astype(f32)
                yield 2 * place + k, jnp.concatenate([edges[0][cut], mid, edges[1][cut]], axis=0)

        @pl.when(has_down & has_up)
        def _():
            @pl.loop(i * HALF, (i + 1) * HALF)
            def _(place):
                for pos, value in carried(place):
                    out_ref[pos] = (own_acc[pos] + value).astype(bf16)

        @pl.when(has_down & ~has_up)
        def _():
            @pl.loop(i * HALF, (i + 1) * HALF)
            def _(place):
                for pos, value in carried(place):
                    out_ref[pos] = value.astype(bf16)

    @pl.when(has_down & ~has_up)
    def _():
        for copy in down_edge + down_mid:
            copy.wait_send()

    @pl.when(has_up)
    def _():
        for copy in up_edge + up_mid:
            copy.wait_send()


def body(sizes, features, cotangent):
    _, cols, rows, chans = features.shape
    wide = rows + 2 * RIM
    chunks, half = cols // BLOCK, cols // 2
    near, far = padded(NEAR * wide), padded(FAR * wide)
    vmem, hbm = (pl.BlockSpec(memory_space=space) for space in (pltpu.VMEM, pltpu.HBM))
    short = lambda *dims: pltpu.VMEM(dims + (chans,), jnp.bfloat16)
    full = lambda *dims: pltpu.VMEM(dims + (chans,), jnp.float32)
    messages = 8 * chunks + 14
    out = pl.pallas_call(
        functools.partial(kernel, sizes),
        out_shape=jax.ShapeDtypeStruct((cols, rows, chans), jnp.bfloat16),
        in_specs=[hbm] * 2,
        out_specs=vmem,
        scratch_shapes=[
            short(cols, rows),
            pltpu.VMEM((cols, rows, cotangent.shape[3]), jnp.bfloat16),
            pltpu.VMEM((cotangent.shape[3], near + far), jnp.bfloat16),
            short(2, half, 2 * RIM),
            short(cols, rows - 2 * RIM),
            short(2, half + RIM, 2 * RIM),
            short(2, half + RIM, 2 * RIM),
            short(cols + 2 * RIM, wide),
            short(half + RIM, wide),
            full(cols + 2 * RIM, wide),
            full(half + RIM, wide),
            pltpu.VMEM((chunks, BLOCK * rows, near), jnp.bfloat16),
            pltpu.VMEM((chunks, BLOCK * rows, far), jnp.bfloat16),
            short(2, RIM, rows),
            short(2, RIM, rows),
            short(2, half + RIM, 2 * RIM),
            short(2, half, 2 * RIM),
            short(2, 2, HALF, 2 * RIM),
            short(2, half, 2 * RIM),
            short(cols, rows - 2 * RIM),
            short(2, half, 2 * RIM),
            short(cols, rows - 2 * RIM),
            full(cols, rows),
            pltpu.SemaphoreType.DMA((2 * chunks,)),
            pltpu.SemaphoreType.DMA((messages,)),
            pltpu.SemaphoreType.DMA((messages,)),
        ],
        cost_estimate=pl.CostEstimate(flops=10**10, bytes_accessed=4 << 20, transcendentals=0),
        compiler_params=pltpu.CompilerParams(
            collective_id=0, has_side_effects=True, vmem_limit_bytes=54250 << 10
        ),
    )(features[0], cotangent[0])
    return out[None]


def solution(mesh):
    spec = P("frame", "lon", "lat", None)
    sizes = tuple(mesh.shape[axis] for axis in ("lon", "lat", "frame"))
    return jax.shard_map(
        functools.partial(body, sizes), mesh=mesh, in_specs=(spec, spec), out_specs=spec, check_vma=False
    )
```

```python
import functools

import jax
import jax.numpy as jnp
from jax import lax
from jax.experimental import pallas as pl
from jax.experimental.pallas import tpu as pltpu
from jax.sharding import PartitionSpec as P

LEVELS = 2
RAD = 4
RIM = 8
ACROSS = 2 * RAD + 1
BLOCK = RIM
HALF = RIM // 2
NEAR = ACROSS + BLOCK - 1
FAR = ACROSS + BLOCK // 2 - 1
MESH = pl.DeviceIdType.MESH


def padded(lanes):
    return -(-lanes // 128) * 128


def spreader(wide):
    near, far = padded(NEAR * wide), padded(FAR * wide)
    shape = (LEVELS * ACROSS * ACROSS, near + far)
    row = lax.broadcasted_iota(jnp.int32, (shape[0], 1), 0)
    fine = row < ACROSS * ACROSS
    row = jnp.where(fine, row, row - ACROSS * ACROSS)
    a = sum((row >= k * ACROSS).astype(jnp.int32) for k in range(1, ACROSS))
    b = row - a * ACROSS
    place = a * wide + jnp.where(fine, RAD + b, near + 2 * b)
    lane = lax.broadcasted_iota(jnp.int32, shape, 1)
    return jnp.where(lane == place, 1.0, 0.0).astype(jnp.bfloat16)


def sheared(spread, rows, shifts):
    parts = [
        pltpu.roll(spread[i * rows : (i + 1) * rows], shift, 1, stride=1, stride_axis=0)
        for i, shift in enumerate(shifts)
    ]
    return jnp.concatenate(parts, axis=0).astype(jnp.bfloat16)


def pair_sum(value):
    rows = value.shape[0]
    odd = lax.broadcasted_iota(jnp.int32, value.shape, 0) % 2 == 1
    return value + jnp.where(odd, pltpu.roll(value, 1, 0), pltpu.roll(value, rows - 1, 0))


def kernel(
    sizes,
    feat_hbm,
    cot_hbm,
    out_ref,
    feat_ref,
    cot_ref,
    spread_ref,
    own_edge,
    own_mid,
    key_edge,
    key_rim,
    key_ext,
    pool,
    near_acc,
    far_acc,
    band_near,
    band_far,
    send_lon,
    recv_lon,
    send_rim,
    recv_rim,
    recv_corner,
    send_edge,
    send_mid,
    recv_edge,
    recv_mid,
    own_acc,
    near_by,
    sent,
    got,
):
    n_lon, n_lat, n_frame = sizes
    cols, rows, chans = feat_ref.shape
    wide = rows + 2 * RIM
    chunks, last = cols // BLOCK, cols // BLOCK - 1
    half = cols // 2
    middle = slice(RIM, rows - RIM)
    scale = chans ** (-0.5)
    f32, bf16 = jnp.float32, jnp.bfloat16
    lon, lat, frame = lax.axis_index("lon"), lax.axis_index("lat"), lax.axis_index("frame")
    has_down, has_up = frame > 0, frame < n_frame - 1
    has_low, has_high = lat > 0, lat < n_lat - 1
    inner = list(range(1, last))

    def lateral(dx, dy):
        return {"lon": lax.rem(lon + dx + n_lon, n_lon), "lat": lat + dy}

    def reaches(dy):
        return {-1: has_low, 0: None, 1: has_high}[dy]

    def when(cond, act):
        if cond is None:
            act()
        else:
            pl.when(cond)(act)

    count = [0]

    def fresh():
        count[0] += 1
        return count[0] - 1

    class Message:
        def __init__(self, src, dst, dx, dy):
            self.key, self.dy = fresh(), dy
            self.copy = lambda: pltpu.make_async_remote_copy(
                src_ref=src,
                dst_ref=dst,
                send_sem=sent.at[self.key],
                recv_sem=got.at[self.key],
                device_id=lateral(dx, dy),
                device_id_type=MESH,
            )

        def start(self):
            when(reaches(self.dy), lambda: self.copy().start())

        def receive(self):
            when(reaches(-self.dy), lambda: self.copy().wait_recv())

        def finish(self):
            when(reaches(self.dy), lambda: self.copy().wait_send())

    def vertical(src, dst, step):
        key = fresh()
        return pltpu.make_async_remote_copy(
            src_ref=src,
            dst_ref=dst,
            send_sem=sent.at[key],
            recv_sem=got.at[key],
            device_id={"frame": frame + step},
            device_id_type=MESH,
        )

    def local(src, dst):
        copies.append(pltpu.make_async_copy(src, dst, near_by.at[len(copies)]))
        return copies[-1]

    copies = []
    at = lambda i: pl.ds(i * BLOCK, BLOCK)
    part = lambda ref, start, size: ref.at[pl.ds(start, size)]
    pairs = lambda ref, side, start: ref.at[side, pl.ds(start, HALF)]
    mids = lambda i: key_ext.at[at(i), pl.ds(2 * RIM, rows - 2 * RIM)]
    both = lambda ref, start: ref.at[:, pl.ds(start, HALF)]

    feat_in = [local(feat_hbm.at[at(i)], feat_ref.at[at(i)]) for i in range(chunks)]
    cot_in = [local(cot_hbm.at[at(i)], cot_ref.at[at(i)]) for i in range(chunks)]

    down_edge = [
        vertical(both(own_edge, i * HALF), both(key_edge, (i + 1) * HALF), -1) for i in range(chunks)
    ]
    down_mid = [
        vertical(own_mid.at[at(i)], mids(i + 1), -1) for i in range(chunks)
    ]
    up_edge = [
        vertical(both(send_edge, i * HALF), both(recv_edge, i * HALF), 1) for i in range(chunks)
    ]
    up_mid = [vertical(send_mid.at[at(i)], recv_mid.at[at(i)], 1) for i in range(chunks)]
    key_lat = [
        [
            Message(pairs(key_edge, side, i * HALF), pairs(key_rim, 1 - side, i * HALF), 0, dy)
            for side, dy in ((0, -1), (1, 1))
        ]
        for i in range(chunks + 2)
    ]

    def key_side(dx):
        begin, end = (HALF, half + HALF) if dx < 0 else (half, 0)
        return [
            Message(mids(2 * begin // BLOCK), mids(2 * end // BLOCK), dx, 0),
            Message(both(key_edge, begin), both(key_edge, end), dx, 0),
        ]

    key_left, key_right = key_side(-1), key_side(1)
    back_lat = [
        [
            Message(pairs(send_rim, side, (i + 1) * HALF), pairs(recv_rim, 1 - side, i * HALF), 0, dy)
            for side, dy in ((0, -1), (1, 1))
        ]
        for i in range(chunks)
    ]

    def back_side(dx):
        side, begin = (0, 0) if dx < 0 else (1, half + HALF)
        return [
            Message(send_lon.at[side], recv_lon.at[side], dx, 0),
            Message(both(send_rim, begin), recv_corner.at[side], dx, 0),
        ]

    back_left, back_right = back_side(-1), back_side(1)

    barrier = pltpu.get_barrier_semaphore()

    def greet(device):
        pl.semaphore_signal(barrier, inc=1, device_id=device, device_id_type=MESH)

    for copy in feat_in:
        copy.start()
    pl.when(has_down)(lambda: greet({"frame": frame - 1}))
    pl.when(has_up)(lambda: greet({"frame": frame + 1}))
    one = lambda cond: jnp.where(cond, 1, 0)

    @pl.when(has_up)
    def _():
        for dx, dy in ((-1, 0), (1, 0), (0, -1), (0, 1)):
            when(reaches(dy), lambda: greet(lateral(dx, dy)))
        for copy in cot_in:
            copy.start()

        for side, present in ((0, has_low), (1, has_high)):

            @pl.when(~present)
            def _():
                key_rim[side] = jnp.zeros(key_rim.shape[1:], bf16)
                recv_rim[side] = jnp.zeros(recv_rim.shape[1:], bf16)

        spread_ref[...] = spreader(wide)

        for begin in (0, cols + 2 * RIM - RAD):
            near_acc[pl.ds(begin, RAD)] = jnp.zeros((RAD, wide, chans), f32)

    for copy in feat_in:
        copy.wait()

    @pl.when(has_down)
    def _():
        @pl.loop(0, half)
        def _(pos):
            first, second = feat_ref[2 * pos].astype(f32), feat_ref[2 * pos + 1].astype(f32)
            low = jnp.concatenate([first[:RIM], second[:RIM]], axis=0)
            high = jnp.concatenate([first[rows - RIM :], second[rows - RIM :]], axis=0)
            own_edge[0, pos] = low.astype(bf16)
            own_edge[1, pos] = high.astype(bf16)
            own_mid[2 * pos] = first[middle].astype(bf16)
            own_mid[2 * pos + 1] = second[middle].astype(bf16)

    lateral_count = 2 + one(has_low) + one(has_high)
    pl.semaphore_wait(barrier, one(has_down) + one(has_up) * (1 + lateral_count))

    @pl.when(has_down)
    def _():
        for i in (0, last):
            down_edge[i].start()
        down_mid[0].start()
        for i in inner:
            down_edge[i].start()
        for i in (last, *inner):
            down_mid[i].start()

    @pl.when(has_up)
    def _():
        def add(ref, start, value, held):
            if held:
                ref[pl.ds(start, held)] += value[:held]
            ref[pl.ds(start + held, value.shape[0] - held)] = value[held:]

        def back(i):
            cot_in[i].wait()
            cot = cot_ref[at(i)].reshape(BLOCK * rows, cot_ref.shape[2])
            spread = jnp.dot(cot, spread_ref[...], preferred_element_type=f32)
            split = band_near.shape[2]
            near = sheared(spread[:, :split], rows, [j * wide for j in range(BLOCK)])
            far = sheared(spread[:, split:], rows, [j // 2 * wide for j in range(BLOCK)])
            band_near[i] = near
            band_far[i] = far
            feats = feat_ref[at(i)].reshape(BLOCK * rows, chans)
            contract = (((0,), (0,)), ((), ()))
            grad = lax.dot_general(near, feats, contract, preferred_element_type=f32)
            grad = grad[: NEAR * wide].reshape(NEAR, wide, chans)
            add(near_acc, i * BLOCK + RAD, grad, i and NEAR - BLOCK)
            grad = lax.dot_general(far, feats, contract, preferred_element_type=f32)
            grad = grad[: FAR * wide].reshape(FAR, wide, chans)
            add(far_acc, i * (BLOCK // 2), grad, i and FAR - BLOCK // 2)

        def settle(pos):
            coarse = pair_sum(far_acc[pos]) * 0.25
            first = (near_acc[2 * pos] + coarse) * scale
            second = (near_acc[2 * pos + 1] + coarse) * scale
            for side, begin in ((0, 0), (1, RIM + rows)):
                cut = slice(begin, begin + RIM)
                send_rim[side, pos] = jnp.concatenate([first[cut], second[cut]], axis=0).astype(bf16)
            return first[RIM : RIM + rows], second[RIM : RIM + rows]

        def settle_side(side):
            @pl.loop(0, HALF)
            def _(pos):
                first, second = settle(pos + side * (half + HALF))
                send_lon[side, 2 * pos] = first.astype(bf16)
                send_lon[side, 2 * pos + 1] = second.astype(bf16)

            for message in (back_left, back_right)[side]:
                message.start()

        def settle_inner(i):
            @pl.loop(0, HALF)
            def _(pos):
                place = i * HALF + pos
                for k, value in enumerate(settle(place + HALF)):
                    near_acc[RIM + 2 * place + k, RIM : RIM + rows] = value
                    if 0 < i < last:
                        send_mid[2 * place + k] = value[middle].astype(bf16)

            if 0 < i < last:
                for message in back_lat[i]:
                    message.start()
                up_mid[i].start()

        def join_corner(i):
            side = int(i == 0)
            for message in (back_left, back_right)[side]:
                message.receive()

            @pl.loop(0, HALF)
            def _(pos):
                for k in range(2):
                    place = (i + 1) * HALF + pos
                    value = send_rim[k, place].astype(f32) + recv_corner[side, k, pos].astype(f32)
                    send_rim[k, place] = value.astype(bf16)

            for message in back_lat[i]:
                message.start()

        def forward_edge(i):
            down_edge[i].wait_recv()
            for message in key_lat[i + 1]:
                message.start()
            if i in (0, last):
                (key_left if i == 0 else key_right)[1].start()

        def forward_side(i):
            (key_right if i == 0 else key_left)[1].receive()
            for message in key_lat[0 if i == 0 else chunks + 1]:
                message.start()

        def forward_mid(i):
            down_mid[i].wait_recv()
            (key_left if i == 0 else key_right)[0].start()

        def rise_edge(i):
            for message in back_lat[i]:
                message.receive()

            @pl.loop(i * HALF, (i + 1) * HALF)
            def _(place):
                for side, begin in ((0, RIM), (1, rows)):
                    value = recv_rim[side, place].astype(f32)
                    own = [
                        near_acc[RIM + 2 * place + k, begin : begin + RIM] for k in range(2)
                    ]
                    value = value + jnp.concatenate(own, axis=0)
                    send_edge[side, place] = value.astype(bf16)

            up_edge[i].start()

        def rise_side(i):
            side = int(i == 0)

            @pl.loop(0, BLOCK)
            def _(pos):
                place = RIM + i * BLOCK + pos
                rim = recv_lon[side, pos].astype(f32)
                value = near_acc[place, RIM : RIM + rows] + rim
                near_acc[place, RIM : RIM + rows] = value
                send_mid[i * BLOCK + pos] = value[middle].astype(bf16)

            up_mid[i].start()

        for i in range(chunks):
            back(i)
            if i == 0:
                settle_side(0)
            elif i > 1:
                settle_inner(i - 1)
        settle_side(1)
        settle_inner(0)
        settle_inner(last)
        join_corner(last)
        forward_edge(0)
        forward_edge(last)
        rise_edge(inner[0])
        rise_edge(inner[1])
        forward_mid(0)
        join_corner(0)
        forward_edge(inner[0])
        rise_side(last)
        rise_edge(last)
        forward_side(0)
        forward_side(last)
        forward_edge(inner[1])
        rise_side(0)
        rise_edge(0)
        forward_mid(last)

        def unfold_edge(i):
            @pl.loop(i * HALF, (i + 1) * HALF)
            def _(pos):
                for side, begin in ((0, 0), (1, rows)):
                    pieces = [ref[side, pos].astype(f32) for ref in (key_rim, key_edge)[:: 1 - 2 * side]]
                    values = []
                    for k in range(2):
                        cut = slice(k * RIM, (k + 1) * RIM)
                        values.append(jnp.concatenate([piece[cut] for piece in pieces], axis=0))
                        key_ext[2 * pos + k, begin : begin + 2 * RIM] = values[k].astype(bf16)
                    pool[pos, begin : begin + 2 * RIM] = pooled(values)

        def unfold_mid(i):
            for pos in range(i * HALF, (i + 1) * HALF):
                values = [key_ext[2 * pos + k, 2 * RIM : rows].astype(f32) for k in range(2)]
                pool[pos, 2 * RIM : rows] = pooled(values)

        def pooled(values):
            return (pair_sum(values[0] + values[1]) * 0.25).astype(bf16)

        def own(i):
            keys = key_ext[pl.ds(i * BLOCK + RAD, NEAR)].reshape(NEAR * wide, chans)
            coarse = pool[pl.ds(i * (BLOCK // 2), FAR)].reshape(FAR * wide, chans)
            total = jnp.dot(band_near[i, :, : NEAR * wide], keys, preferred_element_type=f32)
            total += jnp.dot(band_far[i, :, : FAR * wide], coarse, preferred_element_type=f32)
            total = (total * scale).reshape(BLOCK, rows, chans)
            own_acc[at(i)] = total
            out_ref[at(i)] = total.astype(bf16)

        key_left[0].receive()
        key_right[0].receive()
        for i in (0, 1, chunks, chunks + 1):
            for message in key_lat[i]:
                message.receive()
        for i in (0, 1, last + 1, last + 2):
            unfold_edge(i)
            unfold_mid(i)
        for i in inner:
            for message in key_lat[i + 1]:
                message.receive()
            unfold_edge(i + 1)
            if i == inner[-1]:
                for group in key_lat + back_lat + [key_left, key_right, back_left, back_right]:
                    for message in group:
                        message.finish()

                @pl.when(has_down)
                def _():
                    for copy in down_edge + down_mid:
                        copy.wait_send()

            down_mid[i].wait_recv()
            unfold_mid(i + 1)
            own(i - 1)
        for i in range(inner[-1], chunks):
            own(i)

    for i in inner + [last, 0]:

        @pl.when(has_down)
        def _():
            up_mid[i].wait_recv()
            up_edge[i].wait_recv()

        def carried(place):
            edges = [recv_edge[side, place].astype(f32) for side in range(2)]
            for k in range(2):
                cut = slice(k * RIM, (k + 1) * RIM)
                mid = recv_mid[2 * place + k].astype(f32)
                yield 2 * place + k, jnp.concatenate([edges[0][cut], mid, edges[1][cut]], axis=0)

        @pl.when(has_down & has_up)
        def _():
            @pl.loop(i * HALF, (i + 1) * HALF)
            def _(place):
                for pos, value in carried(place):
                    out_ref[pos] = (own_acc[pos] + value).astype(bf16)

        @pl.when(has_down & ~has_up)
        def _():
            @pl.loop(i * HALF, (i + 1) * HALF)
            def _(place):
                for pos, value in carried(place):
                    out_ref[pos] = value.astype(bf16)

    @pl.when(has_down & ~has_up)
    def _():
        for copy in down_edge + down_mid:
            copy.wait_send()

    @pl.when(has_up)
    def _():
        for copy in up_edge + up_mid:
            copy.wait_send()


def body(sizes, features, cotangent):
    _, cols, rows, chans = features.shape
    wide = rows + 2 * RIM
    chunks, half = cols // BLOCK, cols // 2
    near, far = padded(NEAR * wide), padded(FAR * wide)
    vmem, hbm = (pl.BlockSpec(memory_space=space) for space in (pltpu.VMEM, pltpu.HBM))
    short = lambda *dims: pltpu.VMEM(dims + (chans,), jnp.bfloat16)
    full = lambda *dims: pltpu.VMEM(dims + (chans,), jnp.float32)
    messages = 8 * chunks + 12
    out = pl.pallas_call(
        functools.partial(kernel, sizes),
        out_shape=jax.ShapeDtypeStruct((cols, rows, chans), jnp.bfloat16),
        in_specs=[hbm] * 2,
        out_specs=vmem,
        scratch_shapes=[
            short(cols, rows),
            pltpu.VMEM((cols, rows, cotangent.shape[3]), jnp.bfloat16),
            pltpu.VMEM((cotangent.shape[3], near + far), jnp.bfloat16),
            short(2, half, 2 * RIM),
            short(cols, rows - 2 * RIM),
            short(2, half + RIM, 2 * RIM),
            short(2, half + RIM, 2 * RIM),
            short(cols + 2 * RIM, wide),
            short(half + RIM, wide),
            full(cols + 2 * RIM, wide),
            full(half + RIM, wide),
            pltpu.VMEM((chunks, BLOCK * rows, near), jnp.bfloat16),
            pltpu.VMEM((chunks, BLOCK * rows, far), jnp.bfloat16),
            short(2, RIM, rows),
            short(2, RIM, rows),
            short(2, half + RIM, 2 * RIM),
            short(2, half, 2 * RIM),
            short(2, 2, HALF, 2 * RIM),
            short(2, half, 2 * RIM),
            short(cols, rows - 2 * RIM),
            short(2, half, 2 * RIM),
            short(cols, rows - 2 * RIM),
            full(cols, rows),
            pltpu.SemaphoreType.DMA((2 * chunks,)),
            pltpu.SemaphoreType.DMA((messages,)),
            pltpu.SemaphoreType.DMA((messages,)),
        ],
        cost_estimate=pl.CostEstimate(flops=10**10, bytes_accessed=4 << 20, transcendentals=0),
        compiler_params=pltpu.CompilerParams(
            collective_id=0, has_side_effects=True, vmem_limit_bytes=54250 << 10
        ),
    )(features[0], cotangent[0])
    return out[None]


def solution(mesh):
    spec = P("frame", "lon", "lat", None)
    sizes = tuple(mesh.shape[axis] for axis in ("lon", "lat", "frame"))
    return jax.shard_map(
        functools.partial(body, sizes), mesh=mesh, in_specs=(spec, spec), out_specs=spec, check_vma=False
    )
```

```python
import functools

import jax
import jax.numpy as jnp
from jax import lax
from jax.experimental import pallas as pl
from jax.experimental.pallas import tpu as pltpu
from jax.sharding import PartitionSpec as P

LEVELS = 2
RAD = 4
RIM = 8
ACROSS = 2 * RAD + 1
BLOCK = RIM
HALF = RIM // 2
NEAR = ACROSS + BLOCK - 1
FAR = ACROSS + BLOCK // 2 - 1
MESH = pl.DeviceIdType.MESH


def padded(lanes):
    return -(-lanes // 128) * 128


def spreader(wide):
    near, far = padded(NEAR * wide), padded(FAR * wide)
    shape = (LEVELS * ACROSS * ACROSS, near + far)
    row = lax.broadcasted_iota(jnp.int32, (shape[0], 1), 0)
    fine = row < ACROSS * ACROSS
    row = jnp.where(fine, row, row - ACROSS * ACROSS)
    a = sum((row >= k * ACROSS).astype(jnp.int32) for k in range(1, ACROSS))
    b = row - a * ACROSS
    place = a * wide + jnp.where(fine, RAD + b, near + 2 * b)
    lane = lax.broadcasted_iota(jnp.int32, shape, 1)
    return jnp.where(lane == place, 1.0, 0.0).astype(jnp.bfloat16)


def sheared(spread, rows, shifts):
    parts = [
        pltpu.roll(spread[i * rows : (i + 1) * rows], shift, 1, stride=1, stride_axis=0)
        for i, shift in enumerate(shifts)
    ]
    return jnp.concatenate(parts, axis=0).astype(jnp.bfloat16)


def pair_sum(value):
    rows = value.shape[0]
    odd = lax.broadcasted_iota(jnp.int32, value.shape, 0) % 2 == 1
    return value + jnp.where(odd, pltpu.roll(value, 1, 0), pltpu.roll(value, rows - 1, 0))


def kernel(
    sizes,
    feat_hbm,
    cot_hbm,
    out_ref,
    feat_ref,
    cot_ref,
    spread_ref,
    own_edge,
    own_mid,
    key_edge,
    key_rim,
    key_ext,
    pool,
    near_acc,
    far_acc,
    band_near,
    band_far,
    send_lon,
    recv_lon,
    send_rim,
    recv_rim,
    recv_corner,
    send_edge,
    send_mid,
    recv_edge,
    recv_mid,
    own_acc,
    near_by,
    sent,
    got,
):
    n_lon, n_lat, n_frame = sizes
    cols, rows, chans = feat_ref.shape
    wide = rows + 2 * RIM
    chunks, last = cols // BLOCK, cols // BLOCK - 1
    half = cols // 2
    middle = slice(RIM, rows - RIM)
    scale = chans ** (-0.5)
    f32, bf16 = jnp.float32, jnp.bfloat16
    lon, lat, frame = lax.axis_index("lon"), lax.axis_index("lat"), lax.axis_index("frame")
    has_down, has_up = frame > 0, frame < n_frame - 1
    has_low, has_high = lat > 0, lat < n_lat - 1
    inner = list(range(1, last))

    def lateral(dx, dy):
        return {"lon": lax.rem(lon + dx + n_lon, n_lon), "lat": lat + dy}

    def reaches(dy):
        return {-1: has_low, 0: None, 1: has_high}[dy]

    def when(cond, act):
        if cond is None:
            act()
        else:
            pl.when(cond)(act)

    count = [0]

    def fresh():
        count[0] += 1
        return count[0] - 1

    class Message:
        def __init__(self, src, dst, dx, dy):
            self.key, self.dy = fresh(), dy
            self.copy = lambda: pltpu.make_async_remote_copy(
                src_ref=src,
                dst_ref=dst,
                send_sem=sent.at[self.key],
                recv_sem=got.at[self.key],
                device_id=lateral(dx, dy),
                device_id_type=MESH,
            )

        def start(self):
            when(reaches(self.dy), lambda: self.copy().start())

        def receive(self):
            when(reaches(-self.dy), lambda: self.copy().wait_recv())

        def finish(self):
            when(reaches(self.dy), lambda: self.copy().wait_send())

    def vertical(src, dst, step):
        key = fresh()
        return pltpu.make_async_remote_copy(
            src_ref=src,
            dst_ref=dst,
            send_sem=sent.at[key],
            recv_sem=got.at[key],
            device_id={"frame": frame + step},
            device_id_type=MESH,
        )

    def local(src, dst):
        copies.append(pltpu.make_async_copy(src, dst, near_by.at[len(copies)]))
        return copies[-1]

    copies = []
    at = lambda i: pl.ds(i * BLOCK, BLOCK)
    part = lambda ref, start, size: ref.at[pl.ds(start, size)]
    pairs = lambda ref, side, start: ref.at[side, pl.ds(start, HALF)]
    mids = lambda i: key_ext.at[at(i), pl.ds(2 * RIM, rows - 2 * RIM)]
    both = lambda ref, start: ref.at[:, pl.ds(start, HALF)]

    feat_in = [local(feat_hbm.at[at(i)], feat_ref.at[at(i)]) for i in range(chunks)]
    cot_in = [local(cot_hbm.at[at(i)], cot_ref.at[at(i)]) for i in range(chunks)]

    down_edge = [
        vertical(both(own_edge, i * HALF), both(key_edge, (i + 1) * HALF), -1) for i in range(chunks)
    ]
    down_mid = [
        vertical(own_mid.at[at(i)], mids(i + 1), -1) for i in range(chunks)
    ]
    up_edge = [
        vertical(both(send_edge, i * HALF), both(recv_edge, i * HALF), 1) for i in range(chunks)
    ]
    up_mid = [vertical(send_mid.at[at(i)], recv_mid.at[at(i)], 1) for i in range(chunks)]
    key_lat = [
        [
            Message(pairs(key_edge, side, i * HALF), pairs(key_rim, 1 - side, i * HALF), 0, dy)
            for side, dy in ((0, -1), (1, 1))
        ]
        for i in range(chunks + 2)
    ]

    def key_side(dx):
        begin, end = (HALF, half + HALF) if dx < 0 else (half, 0)
        return [
            Message(mids(2 * begin // BLOCK), mids(2 * end // BLOCK), dx, 0),
            Message(both(key_edge, begin), both(key_edge, end), dx, 0),
        ]

    key_left, key_right = key_side(-1), key_side(1)
    back_lat = [
        [
            Message(pairs(send_rim, side, (i + 1) * HALF), pairs(recv_rim, 1 - side, i * HALF), 0, dy)
            for side, dy in ((0, -1), (1, 1))
        ]
        for i in range(chunks)
    ]

    def back_side(dx):
        side, begin = (0, 0) if dx < 0 else (1, half + HALF)
        return [
            Message(send_lon.at[side], recv_lon.at[side], dx, 0),
            Message(both(send_rim, begin), recv_corner.at[side], dx, 0),
        ]

    back_left, back_right = back_side(-1), back_side(1)

    barrier = pltpu.get_barrier_semaphore()

    def greet(device):
        pl.semaphore_signal(barrier, inc=1, device_id=device, device_id_type=MESH)

    pl.when(has_down)(lambda: greet({"frame": frame - 1}))
    pl.when(has_up)(lambda: greet({"frame": frame + 1}))
    one = lambda cond: jnp.where(cond, 1, 0)

    @pl.when(~has_up)
    def _():
        for copy in feat_in:
            copy.start()

    @pl.when(has_up)
    def _():
        for dx, dy in ((-1, 0), (1, 0), (0, -1), (0, 1)):
            when(reaches(dy), lambda: greet(lateral(dx, dy)))
        for copy in feat_in:
            copy.start()
        for copy in cot_in:
            copy.start()

    for copy in feat_in:
        copy.wait()

    @pl.when(has_down)
    def _():
        @pl.loop(0, half)
        def _(pos):
            first, second = feat_ref[2 * pos].astype(f32), feat_ref[2 * pos + 1].astype(f32)
            low = jnp.concatenate([first[:RIM], second[:RIM]], axis=0)
            high = jnp.concatenate([first[rows - RIM :], second[rows - RIM :]], axis=0)
            own_edge[0, pos] = low.astype(bf16)
            own_edge[1, pos] = high.astype(bf16)
            own_mid[2 * pos] = first[middle].astype(bf16)
            own_mid[2 * pos + 1] = second[middle].astype(bf16)

    lateral_count = 2 + one(has_low) + one(has_high)
    pl.semaphore_wait(barrier, one(has_down) + one(has_up) * (1 + lateral_count))

    @pl.when(has_down)
    def _():
        for i in (0, last):
            down_edge[i].start()
        down_mid[0].start()
        for i in inner:
            down_edge[i].start()
        for i in (last, *inner):
            down_mid[i].start()

    @pl.when(has_up)
    def _():
        for side, present in ((0, has_low), (1, has_high)):

            @pl.when(~present)
            def _():
                key_rim[side] = jnp.zeros(key_rim.shape[1:], bf16)
                recv_rim[side] = jnp.zeros(recv_rim.shape[1:], bf16)

        spread_ref[...] = spreader(wide)

        for begin in (0, cols + 2 * RIM - RAD):
            near_acc[pl.ds(begin, RAD)] = jnp.zeros((RAD, wide, chans), f32)

        def add(ref, start, value, held):
            if held:
                ref[pl.ds(start, held)] += value[:held]
            ref[pl.ds(start + held, value.shape[0] - held)] = value[held:]

        def back(i):
            cot_in[i].wait()
            cot = cot_ref[at(i)].reshape(BLOCK * rows, cot_ref.shape[2])
            spread = jnp.dot(cot, spread_ref[...], preferred_element_type=f32)
            split = band_near.shape[2]
            near = sheared(spread[:, :split], rows, [j * wide for j in range(BLOCK)])
            far = sheared(spread[:, split:], rows, [j // 2 * wide for j in range(BLOCK)])
            band_near[i] = near
            band_far[i] = far
            feats = feat_ref[at(i)].reshape(BLOCK * rows, chans)
            contract = (((0,), (0,)), ((), ()))
            grad = lax.dot_general(near, feats, contract, preferred_element_type=f32)
            grad = grad[: NEAR * wide].reshape(NEAR, wide, chans)
            add(near_acc, i * BLOCK + RAD, grad, i and NEAR - BLOCK)
            grad = lax.dot_general(far, feats, contract, preferred_element_type=f32)
            grad = grad[: FAR * wide].reshape(FAR, wide, chans)
            add(far_acc, i * (BLOCK // 2), grad, i and FAR - BLOCK // 2)

        def settle(pos):
            coarse = pair_sum(far_acc[pos]) * 0.25
            first = (near_acc[2 * pos] + coarse) * scale
            second = (near_acc[2 * pos + 1] + coarse) * scale
            for side, begin in ((0, 0), (1, RIM + rows)):
                cut = slice(begin, begin + RIM)
                send_rim[side, pos] = jnp.concatenate([first[cut], second[cut]], axis=0).astype(bf16)
            return first[RIM : RIM + rows], second[RIM : RIM + rows]

        def settle_side(side):
            @pl.loop(0, HALF, unroll=True)
            def _(pos):
                first, second = settle(pos + side * (half + HALF))
                send_lon[side, 2 * pos] = first.astype(bf16)
                send_lon[side, 2 * pos + 1] = second.astype(bf16)

            for message in (back_left, back_right)[side]:
                message.start()

        def settle_inner(i):
            @pl.loop(0, HALF, unroll=True)
            def _(pos):
                place = i * HALF + pos
                for k, value in enumerate(settle(place + HALF)):
                    near_acc[RIM + 2 * place + k, RIM : RIM + rows] = value
                    if 0 < i < last:
                        send_mid[2 * place + k] = value[middle].astype(bf16)

            if 0 < i < last:
                for message in back_lat[i]:
                    message.start()
                up_mid[i].start()

        def join_corner(i):
            side = int(i == 0)
            for message in (back_left, back_right)[side]:
                message.receive()

            @pl.loop(0, HALF, unroll=True)
            def _(pos):
                for k in range(2):
                    place = (i + 1) * HALF + pos
                    value = send_rim[k, place].astype(f32) + recv_corner[side, k, pos].astype(f32)
                    send_rim[k, place] = value.astype(bf16)

            for message in back_lat[i]:
                message.start()

        def forward_edge(i):
            down_edge[i].wait_recv()
            for message in key_lat[i + 1]:
                message.start()
            if i in (0, last):
                (key_left if i == 0 else key_right)[1].start()

        def forward_side(i):
            (key_right if i == 0 else key_left)[1].receive()
            for message in key_lat[0 if i == 0 else chunks + 1]:
                message.start()

        def forward_mid(i):
            down_mid[i].wait_recv()
            (key_left if i == 0 else key_right)[0].start()

        def rise_edge(i):
            for message in back_lat[i]:
                message.receive()

            @pl.loop(i * HALF, (i + 1) * HALF, unroll=True)
            def _(place):
                for side, begin in ((0, RIM), (1, rows)):
                    value = recv_rim[side, place].astype(f32)
                    own = [
                        near_acc[RIM + 2 * place + k, begin : begin + RIM] for k in range(2)
                    ]
                    value = value + jnp.concatenate(own, axis=0)
                    send_edge[side, place] = value.astype(bf16)

            up_edge[i].start()

        def rise_side(i):
            side = int(i == 0)

            @pl.loop(0, BLOCK)
            def _(pos):
                place = RIM + i * BLOCK + pos
                rim = recv_lon[side, pos].astype(f32)
                value = near_acc[place, RIM : RIM + rows] + rim
                near_acc[place, RIM : RIM + rows] = value
                send_mid[i * BLOCK + pos] = value[middle].astype(bf16)

            up_mid[i].start()

        for i in range(chunks):
            back(i)
            if i == 0:
                settle_side(0)
            elif i > 1:
                settle_inner(i - 1)
        settle_side(1)
        settle_inner(0)
        settle_inner(last)
        join_corner(last)
        forward_edge(0)
        forward_edge(last)
        rise_edge(inner[0])
        rise_edge(inner[1])
        forward_mid(0)
        join_corner(0)
        forward_edge(inner[0])
        rise_side(last)
        rise_edge(last)
        forward_side(0)
        forward_side(last)
        forward_edge(inner[1])
        rise_side(0)
        rise_edge(0)
        forward_mid(last)

        def unfold_edge(i):
            @pl.loop(i * HALF, (i + 1) * HALF, unroll=True)
            def _(pos):
                for side, begin in ((0, 0), (1, rows)):
                    pieces = [ref[side, pos].astype(f32) for ref in (key_rim, key_edge)[:: 1 - 2 * side]]
                    values = []
                    for k in range(2):
                        cut = slice(k * RIM, (k + 1) * RIM)
                        values.append(jnp.concatenate([piece[cut] for piece in pieces], axis=0))
                        key_ext[2 * pos + k, begin : begin + 2 * RIM] = values[k].astype(bf16)
                    pool[pos, begin : begin + 2 * RIM] = pooled(values)

        def unfold_mid(i):
            for pos in range(i * HALF, (i + 1) * HALF):
                values = [key_ext[2 * pos + k, 2 * RIM : rows].astype(f32) for k in range(2)]
                pool[pos, 2 * RIM : rows] = pooled(values)

        def pooled(values):
            return (pair_sum(values[0] + values[1]) * 0.25).astype(bf16)

        def own(i):
            keys = key_ext[pl.ds(i * BLOCK + RAD, NEAR)].reshape(NEAR * wide, chans)
            coarse = pool[pl.ds(i * (BLOCK // 2), FAR)].reshape(FAR * wide, chans)
            total = jnp.dot(band_near[i, :, : NEAR * wide], keys, preferred_element_type=f32)
            total += jnp.dot(band_far[i, :, : FAR * wide], coarse, preferred_element_type=f32)
            total = (total * scale).reshape(BLOCK, rows, chans)
            own_acc[at(i)] = total
            out_ref[at(i)] = total.astype(bf16)

        key_left[0].receive()
        key_right[0].receive()
        for i in (0, 1, chunks, chunks + 1):
            for message in key_lat[i]:
                message.receive()
        for i in (0, 1, last + 1, last + 2):
            unfold_edge(i)
            unfold_mid(i)
        for i in inner:
            for message in key_lat[i + 1]:
                message.receive()
            unfold_edge(i + 1)
            if i == inner[-1]:
                for group in key_lat + back_lat + [key_left, key_right, back_left, back_right]:
                    for message in group:
                        message.finish()

                @pl.when(has_down)
                def _():
                    for copy in down_edge + down_mid:
                        copy.wait_send()

            down_mid[i].wait_recv()
            unfold_mid(i + 1)
            own(i - 1)
        for i in range(inner[-1], chunks):
            own(i)

    for i in inner + [last, 0]:

        @pl.when(has_down)
        def _():
            up_mid[i].wait_recv()
            up_edge[i].wait_recv()

        def carried(place):
            edges = [recv_edge[side, place].astype(f32) for side in range(2)]
            for k in range(2):
                cut = slice(k * RIM, (k + 1) * RIM)
                mid = recv_mid[2 * place + k].astype(f32)
                yield 2 * place + k, jnp.concatenate([edges[0][cut], mid, edges[1][cut]], axis=0)

        @pl.when(has_down & has_up)
        def _():
            @pl.loop(i * HALF, (i + 1) * HALF, unroll=True)
            def _(place):
                for pos, value in carried(place):
                    out_ref[pos] = (own_acc[pos] + value).astype(bf16)

        @pl.when(has_down & ~has_up)
        def _():
            @pl.loop(i * HALF, (i + 1) * HALF, unroll=True)
            def _(place):
                for pos, value in carried(place):
                    out_ref[pos] = value.astype(bf16)

    @pl.when(has_down & ~has_up)
    def _():
        for copy in down_edge + down_mid:
            copy.wait_send()

    @pl.when(has_up)
    def _():
        for copy in up_edge + up_mid:
            copy.wait_send()


def body(sizes, features, cotangent):
    _, cols, rows, chans = features.shape
    wide = rows + 2 * RIM
    chunks, half = cols // BLOCK, cols // 2
    near, far = padded(NEAR * wide), padded(FAR * wide)
    vmem, hbm = (pl.BlockSpec(memory_space=space) for space in (pltpu.VMEM, pltpu.HBM))
    short = lambda *dims: pltpu.VMEM(dims + (chans,), jnp.bfloat16)
    full = lambda *dims: pltpu.VMEM(dims + (chans,), jnp.float32)
    messages = 8 * chunks + 12
    out = pl.pallas_call(
        functools.partial(kernel, sizes),
        out_shape=jax.ShapeDtypeStruct((cols, rows, chans), jnp.bfloat16),
        in_specs=[hbm] * 2,
        out_specs=vmem,
        scratch_shapes=[
            short(cols, rows),
            pltpu.VMEM((cols, rows, cotangent.shape[3]), jnp.bfloat16),
            pltpu.VMEM((cotangent.shape[3], near + far), jnp.bfloat16),
            short(2, half, 2 * RIM),
            short(cols, rows - 2 * RIM),
            short(2, half + RIM, 2 * RIM),
            short(2, half + RIM, 2 * RIM),
            short(cols + 2 * RIM, wide),
            short(half + RIM, wide),
            full(cols + 2 * RIM, wide),
            full(half + RIM, wide),
            pltpu.VMEM((chunks, BLOCK * rows, near), jnp.bfloat16),
            pltpu.VMEM((chunks, BLOCK * rows, far), jnp.bfloat16),
            short(2, RIM, rows),
            short(2, RIM, rows),
            short(2, half + RIM, 2 * RIM),
            short(2, half, 2 * RIM),
            short(2, 2, HALF, 2 * RIM),
            short(2, half, 2 * RIM),
            short(cols, rows - 2 * RIM),
            short(2, half, 2 * RIM),
            short(cols, rows - 2 * RIM),
            full(cols, rows),
            pltpu.SemaphoreType.DMA((2 * chunks,)),
            pltpu.SemaphoreType.DMA((messages,)),
            pltpu.SemaphoreType.DMA((messages,)),
        ],
        cost_estimate=pl.CostEstimate(flops=10**10, bytes_accessed=4 << 20, transcendentals=0),
        compiler_params=pltpu.CompilerParams(
            collective_id=0, has_side_effects=True, vmem_limit_bytes=54250 << 10
        ),
    )(features[0], cotangent[0])
    return out[None]


def solution(mesh):
    spec = P("frame", "lon", "lat", None)
    sizes = tuple(mesh.shape[axis] for axis in ("lon", "lat", "frame"))
    return jax.shard_map(
        functools.partial(body, sizes), mesh=mesh, in_specs=(spec, spec), out_specs=spec, check_vma=False
    )
```

```python
import functools

import jax
import jax.numpy as jnp
from jax import lax
from jax.experimental import pallas as pl
from jax.experimental.pallas import tpu as pltpu
from jax.sharding import PartitionSpec as P

LEVELS = 2
RAD = 4
RIM = 8
ACROSS = 2 * RAD + 1
BLOCK = RIM
HALF = RIM // 2
NEAR = ACROSS + BLOCK - 1
FAR = ACROSS + BLOCK // 2 - 1
MESH = pl.DeviceIdType.MESH


def padded(lanes):
    return -(-lanes // 128) * 128


def spreader(wide):
    near, far = padded(NEAR * wide), padded(FAR * wide)
    shape = (LEVELS * ACROSS * ACROSS, near + far)
    row = lax.broadcasted_iota(jnp.int32, (shape[0], 1), 0)
    fine = row < ACROSS * ACROSS
    row = jnp.where(fine, row, row - ACROSS * ACROSS)
    a = sum((row >= k * ACROSS).astype(jnp.int32) for k in range(1, ACROSS))
    b = row - a * ACROSS
    place = a * wide + jnp.where(fine, RAD + b, near + 2 * b)
    lane = lax.broadcasted_iota(jnp.int32, shape, 1)
    return jnp.where(lane == place, 1.0, 0.0).astype(jnp.bfloat16)


def sheared(spread, rows, shifts):
    parts = [
        pltpu.roll(spread[i * rows : (i + 1) * rows], shift, 1, stride=1, stride_axis=0)
        for i, shift in enumerate(shifts)
    ]
    return jnp.concatenate(parts, axis=0).astype(jnp.bfloat16)


def pair_sum(value):
    rows = value.shape[0]
    odd = lax.broadcasted_iota(jnp.int32, value.shape, 0) % 2 == 1
    return value + jnp.where(odd, pltpu.roll(value, 1, 0), pltpu.roll(value, rows - 1, 0))


def kernel(
    sizes,
    feat_hbm,
    cot_hbm,
    out_ref,
    feat_ref,
    cot_ref,
    spread_ref,
    own_edge,
    own_mid,
    key_edge,
    key_rim,
    key_ext,
    pool,
    near_acc,
    far_acc,
    band_near,
    band_far,
    send_lon,
    recv_lon,
    send_rim,
    recv_rim,
    recv_corner,
    send_edge,
    send_mid,
    recv_edge,
    recv_mid,
    own_acc,
    near_by,
    sent,
    got,
):
    n_lon, n_lat, n_frame = sizes
    cols, rows, chans = feat_ref.shape
    wide = rows + 2 * RIM
    chunks, last = cols // BLOCK, cols // BLOCK - 1
    half = cols // 2
    middle = slice(RIM, rows - RIM)
    scale = chans ** (-0.5)
    f32, bf16 = jnp.float32, jnp.bfloat16
    lon, lat, frame = lax.axis_index("lon"), lax.axis_index("lat"), lax.axis_index("frame")
    has_down, has_up = frame > 0, frame < n_frame - 1
    has_low, has_high = lat > 0, lat < n_lat - 1
    inner = list(range(1, last))

    def lateral(dx, dy):
        return {"lon": lax.rem(lon + dx + n_lon, n_lon), "lat": lat + dy}

    def reaches(dy):
        return {-1: has_low, 0: None, 1: has_high}[dy]

    def when(cond, act):
        if cond is None:
            act()
        else:
            pl.when(cond)(act)

    count = [0]

    def fresh():
        count[0] += 1
        return count[0] - 1

    class Message:
        def __init__(self, src, dst, dx, dy):
            self.key, self.dy = fresh(), dy
            self.copy = lambda: pltpu.make_async_remote_copy(
                src_ref=src,
                dst_ref=dst,
                send_sem=sent.at[self.key],
                recv_sem=got.at[self.key],
                device_id=lateral(dx, dy),
                device_id_type=MESH,
            )

        def start(self):
            when(reaches(self.dy), lambda: self.copy().start())

        def receive(self):
            when(reaches(-self.dy), lambda: self.copy().wait_recv())

        def finish(self):
            when(reaches(self.dy), lambda: self.copy().wait_send())

    def vertical(src, dst, step):
        key = fresh()
        return pltpu.make_async_remote_copy(
            src_ref=src,
            dst_ref=dst,
            send_sem=sent.at[key],
            recv_sem=got.at[key],
            device_id={"frame": frame + step},
            device_id_type=MESH,
        )

    def local(src, dst):
        copies.append(pltpu.make_async_copy(src, dst, near_by.at[len(copies)]))
        return copies[-1]

    copies = []
    at = lambda i: pl.ds(i * BLOCK, BLOCK)
    part = lambda ref, start, size: ref.at[pl.ds(start, size)]
    pairs = lambda ref, side, start: ref.at[side, pl.ds(start, HALF)]
    mids = lambda i: key_ext.at[at(i), pl.ds(2 * RIM, rows - 2 * RIM)]
    both = lambda ref, start: ref.at[:, pl.ds(start, HALF)]

    feat_in = [local(feat_hbm.at[at(i)], feat_ref.at[at(i)]) for i in range(chunks)]
    cot_in = [local(cot_hbm.at[at(i)], cot_ref.at[at(i)]) for i in range(chunks)]

    down_edge = [
        vertical(both(own_edge, i * HALF), both(key_edge, (i + 1) * HALF), -1) for i in range(chunks)
    ]
    down_mid = [
        vertical(own_mid.at[at(i)], mids(i + 1), -1) for i in range(chunks)
    ]
    up_edge = [
        vertical(both(send_edge, i * HALF), both(recv_edge, i * HALF), 1) for i in range(chunks)
    ]
    up_mid = [vertical(send_mid.at[at(i)], recv_mid.at[at(i)], 1) for i in range(chunks)]
    key_lat = [
        [
            Message(pairs(key_edge, side, i * HALF), pairs(key_rim, 1 - side, i * HALF), 0, dy)
            for side, dy in ((0, -1), (1, 1))
        ]
        for i in range(chunks + 2)
    ]

    def key_side(dx):
        begin, end = (HALF, half + HALF) if dx < 0 else (half, 0)
        return [
            Message(mids(2 * begin // BLOCK), mids(2 * end // BLOCK), dx, 0),
            Message(both(key_edge, begin), both(key_edge, end), dx, 0),
        ]

    key_left, key_right = key_side(-1), key_side(1)
    back_lat = [
        [
            Message(pairs(send_rim, side, (i + 1) * HALF), pairs(recv_rim, 1 - side, i * HALF), 0, dy)
            for side, dy in ((0, -1), (1, 1))
        ]
        for i in range(chunks)
    ]

    def back_side(dx):
        side, begin = (0, 0) if dx < 0 else (1, half + HALF)
        return [
            Message(send_lon.at[side], recv_lon.at[side], dx, 0),
            Message(both(send_rim, begin), recv_corner.at[side], dx, 0),
        ]

    back_left, back_right = back_side(-1), back_side(1)

    barrier = pltpu.get_barrier_semaphore()

    def greet(device):
        pl.semaphore_signal(barrier, inc=1, device_id=device, device_id_type=MESH)

    pl.when(has_down)(lambda: greet({"frame": frame - 1}))
    pl.when(has_up)(lambda: greet({"frame": frame + 1}))
    one = lambda cond: jnp.where(cond, 1, 0)

    @pl.when(~has_up)
    def _():
        for copy in feat_in:
            copy.start()

    @pl.when(has_up)
    def _():
        for dx, dy in ((-1, 0), (1, 0), (0, -1), (0, 1)):
            when(reaches(dy), lambda: greet(lateral(dx, dy)))
        for copy in feat_in:
            copy.start()
        for copy in cot_in:
            copy.start()

    for copy in feat_in:
        copy.wait()

    @pl.when(has_down)
    def _():
        @pl.loop(0, half)
        def _(pos):
            first, second = feat_ref[2 * pos].astype(f32), feat_ref[2 * pos + 1].astype(f32)
            low = jnp.concatenate([first[:RIM], second[:RIM]], axis=0)
            high = jnp.concatenate([first[rows - RIM :], second[rows - RIM :]], axis=0)
            own_edge[0, pos] = low.astype(bf16)
            own_edge[1, pos] = high.astype(bf16)
            own_mid[2 * pos] = first[middle].astype(bf16)
            own_mid[2 * pos + 1] = second[middle].astype(bf16)

    lateral_count = 2 + one(has_low) + one(has_high)
    pl.semaphore_wait(barrier, one(has_down) + one(has_up) * (1 + lateral_count))

    @pl.when(has_down)
    def _():
        for i in (0, last, inner[0]):
            down_edge[i].start()
        down_mid[0].start()
        for i in inner[1:]:
            down_edge[i].start()
        for i in (last, *inner):
            down_mid[i].start()

    @pl.when(has_up)
    def _():
        for side, present in ((0, has_low), (1, has_high)):

            @pl.when(~present)
            def _():
                key_rim[side] = jnp.zeros(key_rim.shape[1:], bf16)
                recv_rim[side] = jnp.zeros(recv_rim.shape[1:], bf16)

        spread_ref[...] = spreader(wide)

        for begin in (0, cols + 2 * RIM - RAD):
            near_acc[pl.ds(begin, RAD)] = jnp.zeros((RAD, wide, chans), f32)

        def add(ref, start, value, held):
            if held:
                ref[pl.ds(start, held)] += value[:held]
            ref[pl.ds(start + held, value.shape[0] - held)] = value[held:]

        def back(i):
            cot_in[i].wait()
            cot = cot_ref[at(i)].reshape(BLOCK * rows, cot_ref.shape[2])
            spread = jnp.dot(cot, spread_ref[...], preferred_element_type=f32)
            split = band_near.shape[2]
            near = sheared(spread[:, :split], rows, [j * wide for j in range(BLOCK)])
            far = sheared(spread[:, split:], rows, [j // 2 * wide for j in range(BLOCK)])
            band_near[i] = near
            band_far[i] = far
            feats = feat_ref[at(i)].reshape(BLOCK * rows, chans)
            contract = (((0,), (0,)), ((), ()))
            grad = lax.dot_general(near, feats, contract, preferred_element_type=f32)
            grad = grad[: NEAR * wide].reshape(NEAR, wide, chans)
            add(near_acc, i * BLOCK + RAD, grad, i and NEAR - BLOCK)
            grad = lax.dot_general(far, feats, contract, preferred_element_type=f32)
            grad = grad[: FAR * wide].reshape(FAR, wide, chans)
            add(far_acc, i * (BLOCK // 2), grad, i and FAR - BLOCK // 2)

        def settle(pos):
            coarse = pair_sum(far_acc[pos]) * 0.25
            first = (near_acc[2 * pos] + coarse) * scale
            second = (near_acc[2 * pos + 1] + coarse) * scale
            for side, begin in ((0, 0), (1, RIM + rows)):
                cut = slice(begin, begin + RIM)
                send_rim[side, pos] = jnp.concatenate([first[cut], second[cut]], axis=0).astype(bf16)
            return first[RIM : RIM + rows], second[RIM : RIM + rows]

        def settle_side(side):
            @pl.loop(0, HALF, unroll=True)
            def _(pos):
                first, second = settle(pos + side * (half + HALF))
                send_lon[side, 2 * pos] = first.astype(bf16)
                send_lon[side, 2 * pos + 1] = second.astype(bf16)

            for message in (back_left, back_right)[side]:
                message.start()

        def settle_inner(i):
            @pl.loop(0, HALF, unroll=True)
            def _(pos):
                place = i * HALF + pos
                for k, value in enumerate(settle(place + HALF)):
                    near_acc[RIM + 2 * place + k, RIM : RIM + rows] = value
                    if 0 < i < last:
                        send_mid[2 * place + k] = value[middle].astype(bf16)

            if 0 < i < last:
                for message in back_lat[i]:
                    message.start()
                up_mid[i].start()

        def join_corner(i):
            side = int(i == 0)
            for message in (back_left, back_right)[side]:
                message.receive()

            @pl.loop(0, HALF, unroll=True)
            def _(pos):
                for k in range(2):
                    place = (i + 1) * HALF + pos
                    value = send_rim[k, place].astype(f32) + recv_corner[side, k, pos].astype(f32)
                    send_rim[k, place] = value.astype(bf16)

            for message in back_lat[i]:
                message.start()

        def forward_edge(i):
            down_edge[i].wait_recv()
            for message in key_lat[i + 1]:
                message.start()
            if i in (0, last):
                (key_left if i == 0 else key_right)[1].start()

        def forward_side(i):
            (key_right if i == 0 else key_left)[1].receive()
            for message in key_lat[0 if i == 0 else chunks + 1]:
                message.start()

        def forward_mid(i):
            down_mid[i].wait_recv()
            (key_left if i == 0 else key_right)[0].start()

        def rise_edge(i):
            for message in back_lat[i]:
                message.receive()

            @pl.loop(i * HALF, (i + 1) * HALF, unroll=True)
            def _(place):
                for side, begin in ((0, RIM), (1, rows)):
                    value = recv_rim[side, place].astype(f32)
                    own = [
                        near_acc[RIM + 2 * place + k, begin : begin + RIM] for k in range(2)
                    ]
                    value = value + jnp.concatenate(own, axis=0)
                    send_edge[side, place] = value.astype(bf16)

            up_edge[i].start()

        def rise_side(i):
            side = int(i == 0)

            @pl.loop(0, BLOCK)
            def _(pos):
                place = RIM + i * BLOCK + pos
                rim = recv_lon[side, pos].astype(f32)
                value = near_acc[place, RIM : RIM + rows] + rim
                near_acc[place, RIM : RIM + rows] = value
                send_mid[i * BLOCK + pos] = value[middle].astype(bf16)

            up_mid[i].start()

        for i in range(chunks):
            back(i)
            if i == 0:
                settle_side(0)
            elif i > 1:
                settle_inner(i - 1)
        settle_side(1)
        settle_inner(0)
        settle_inner(last)
        join_corner(last)
        forward_edge(0)
        forward_edge(last)
        rise_edge(inner[0])
        rise_edge(inner[1])
        forward_edge(inner[0])
        join_corner(0)
        forward_mid(0)
        rise_side(last)
        rise_edge(last)
        forward_side(0)
        forward_side(last)
        forward_edge(inner[1])
        rise_side(0)
        rise_edge(0)
        forward_mid(last)

        def unfold_edge(i):
            @pl.loop(i * HALF, (i + 1) * HALF, unroll=True)
            def _(pos):
                for side, begin in ((0, 0), (1, rows)):
                    pieces = [ref[side, pos].astype(f32) for ref in (key_rim, key_edge)[:: 1 - 2 * side]]
                    values = []
                    for k in range(2):
                        cut = slice(k * RIM, (k + 1) * RIM)
                        values.append(jnp.concatenate([piece[cut] for piece in pieces], axis=0))
                        key_ext[2 * pos + k, begin : begin + 2 * RIM] = values[k].astype(bf16)
                    pool[pos, begin : begin + 2 * RIM] = pooled(values)

        def unfold_mid(i):
            for pos in range(i * HALF, (i + 1) * HALF):
                values = [key_ext[2 * pos + k, 2 * RIM : rows].astype(f32) for k in range(2)]
                pool[pos, 2 * RIM : rows] = pooled(values)

        def pooled(values):
            return (pair_sum(values[0] + values[1]) * 0.25).astype(bf16)

        def own(i):
            keys = key_ext[pl.ds(i * BLOCK + RAD, NEAR)].reshape(NEAR * wide, chans)
            coarse = pool[pl.ds(i * (BLOCK // 2), FAR)].reshape(FAR * wide, chans)
            total = jnp.dot(band_near[i, :, : NEAR * wide], keys, preferred_element_type=f32)
            total += jnp.dot(band_far[i, :, : FAR * wide], coarse, preferred_element_type=f32)
            total = (total * scale).reshape(BLOCK, rows, chans)
            own_acc[at(i)] = total
            out_ref[at(i)] = total.astype(bf16)

        key_left[0].receive()
        key_right[0].receive()
        for i in (0, 1, chunks, chunks + 1):
            for message in key_lat[i]:
                message.receive()
        for i in (0, 1, last + 1, last + 2):
            unfold_edge(i)
            unfold_mid(i)
        for i in inner:
            for message in key_lat[i + 1]:
                message.receive()
            unfold_edge(i + 1)
            if i == inner[-1]:
                for group in key_lat + back_lat + [key_left, key_right, back_left, back_right]:
                    for message in group:
                        message.finish()

                @pl.when(has_down)
                def _():
                    for copy in down_edge + down_mid:
                        copy.wait_send()

            down_mid[i].wait_recv()
            unfold_mid(i + 1)
            own(i - 1)
        for i in range(inner[-1], chunks):
            own(i)

    for i in inner + [last, 0]:

        @pl.when(has_down)
        def _():
            up_mid[i].wait_recv()
            up_edge[i].wait_recv()

        def carried(place):
            edges = [recv_edge[side, place].astype(f32) for side in range(2)]
            for k in range(2):
                cut = slice(k * RIM, (k + 1) * RIM)
                mid = recv_mid[2 * place + k].astype(f32)
                yield 2 * place + k, jnp.concatenate([edges[0][cut], mid, edges[1][cut]], axis=0)

        @pl.when(has_down & has_up)
        def _():
            @pl.loop(i * HALF, (i + 1) * HALF, unroll=True)
            def _(place):
                for pos, value in carried(place):
                    out_ref[pos] = (own_acc[pos] + value).astype(bf16)

        @pl.when(has_down & ~has_up)
        def _():
            @pl.loop(i * HALF, (i + 1) * HALF, unroll=True)
            def _(place):
                for pos, value in carried(place):
                    out_ref[pos] = value.astype(bf16)

    @pl.when(has_down & ~has_up)
    def _():
        for copy in down_edge + down_mid:
            copy.wait_send()

    @pl.when(has_up)
    def _():
        for copy in up_edge + up_mid:
            copy.wait_send()


def body(sizes, features, cotangent):
    _, cols, rows, chans = features.shape
    wide = rows + 2 * RIM
    chunks, half = cols // BLOCK, cols // 2
    near, far = padded(NEAR * wide), padded(FAR * wide)
    vmem, hbm = (pl.BlockSpec(memory_space=space) for space in (pltpu.VMEM, pltpu.HBM))
    short = lambda *dims: pltpu.VMEM(dims + (chans,), jnp.bfloat16)
    full = lambda *dims: pltpu.VMEM(dims + (chans,), jnp.float32)
    messages = 8 * chunks + 12
    out = pl.pallas_call(
        functools.partial(kernel, sizes),
        out_shape=jax.ShapeDtypeStruct((cols, rows, chans), jnp.bfloat16),
        in_specs=[hbm] * 2,
        out_specs=vmem,
        scratch_shapes=[
            short(cols, rows),
            pltpu.VMEM((cols, rows, cotangent.shape[3]), jnp.bfloat16),
            pltpu.VMEM((cotangent.shape[3], near + far), jnp.bfloat16),
            short(2, half, 2 * RIM),
            short(cols, rows - 2 * RIM),
            short(2, half + RIM, 2 * RIM),
            short(2, half + RIM, 2 * RIM),
            short(cols + 2 * RIM, wide),
            short(half + RIM, wide),
            full(cols + 2 * RIM, wide),
            full(half + RIM, wide),
            pltpu.VMEM((chunks, BLOCK * rows, near), jnp.bfloat16),
            pltpu.VMEM((chunks, BLOCK * rows, far), jnp.bfloat16),
            short(2, RIM, rows),
            short(2, RIM, rows),
            short(2, half + RIM, 2 * RIM),
            short(2, half, 2 * RIM),
            short(2, 2, HALF, 2 * RIM),
            short(2, half, 2 * RIM),
            short(cols, rows - 2 * RIM),
            short(2, half, 2 * RIM),
            short(cols, rows - 2 * RIM),
            full(cols, rows),
            pltpu.SemaphoreType.DMA((2 * chunks,)),
            pltpu.SemaphoreType.DMA((messages,)),
            pltpu.SemaphoreType.DMA((messages,)),
        ],
        cost_estimate=pl.CostEstimate(flops=10**10, bytes_accessed=4 << 20, transcendentals=0),
        compiler_params=pltpu.CompilerParams(
            collective_id=0, has_side_effects=True, vmem_limit_bytes=54250 << 10
        ),
    )(features[0], cotangent[0])
    return out[None]


def solution(mesh):
    spec = P("frame", "lon", "lat", None)
    sizes = tuple(mesh.shape[axis] for axis in ("lon", "lat", "frame"))
    return jax.shard_map(
        functools.partial(body, sizes), mesh=mesh, in_specs=(spec, spec), out_specs=spec, check_vma=False
    )
```

```python
import functools

import jax
import jax.numpy as jnp
from jax import lax
from jax.experimental import pallas as pl
from jax.experimental.pallas import tpu as pltpu
from jax.sharding import PartitionSpec as P

LEVELS = 2
RAD = 4
RIM = 8
ACROSS = 2 * RAD + 1
BLOCK = RIM
HALF = RIM // 2
NEAR = ACROSS + BLOCK - 1
FAR = ACROSS + BLOCK // 2 - 1
MESH = pl.DeviceIdType.MESH


def padded(lanes):
    return -(-lanes // 128) * 128


def spreader(wide):
    near, far = padded(NEAR * wide), padded(FAR * wide)
    shape = (LEVELS * ACROSS * ACROSS, near + far)
    row = lax.broadcasted_iota(jnp.int32, (shape[0], 1), 0)
    fine = row < ACROSS * ACROSS
    row = jnp.where(fine, row, row - ACROSS * ACROSS)
    a = sum((row >= k * ACROSS).astype(jnp.int32) for k in range(1, ACROSS))
    b = row - a * ACROSS
    place = a * wide + jnp.where(fine, RAD + b, near + 2 * b)
    lane = lax.broadcasted_iota(jnp.int32, shape, 1)
    return jnp.where(lane == place, 1.0, 0.0).astype(jnp.bfloat16)


def sheared(spread, rows, shifts):
    parts = [
        pltpu.roll(spread[i * rows : (i + 1) * rows], shift, 1, stride=1, stride_axis=0)
        for i, shift in enumerate(shifts)
    ]
    return jnp.concatenate(parts, axis=0).astype(jnp.bfloat16)


def pair_sum(value):
    rows = value.shape[0]
    odd = lax.broadcasted_iota(jnp.int32, value.shape, 0) % 2 == 1
    return value + jnp.where(odd, pltpu.roll(value, 1, 0), pltpu.roll(value, rows - 1, 0))


def kernel(
    sizes,
    feat_hbm,
    cot_hbm,
    out_ref,
    feat_ref,
    cot_ref,
    spread_ref,
    own_edge,
    own_mid,
    key_edge,
    key_rim,
    key_ext,
    pool,
    near_acc,
    far_acc,
    band_near,
    band_far,
    send_lon,
    recv_lon,
    send_rim,
    recv_rim,
    recv_corner,
    send_edge,
    send_mid,
    recv_edge,
    recv_mid,
    own_acc,
    near_by,
    sent,
    got,
):
    n_lon, n_lat, n_frame = sizes
    cols, rows, chans = feat_ref.shape
    wide = rows + 2 * RIM
    chunks, last = cols // BLOCK, cols // BLOCK - 1
    half = cols // 2
    middle = slice(RIM, rows - RIM)
    scale = chans ** (-0.5)
    f32, bf16 = jnp.float32, jnp.bfloat16
    lon, lat, frame = lax.axis_index("lon"), lax.axis_index("lat"), lax.axis_index("frame")
    has_down, has_up = frame > 0, frame < n_frame - 1
    has_low, has_high = lat > 0, lat < n_lat - 1
    inner = list(range(1, last))

    def lateral(dx, dy):
        return {"lon": lax.rem(lon + dx + n_lon, n_lon), "lat": lat + dy}

    def reaches(dy):
        return {-1: has_low, 0: None, 1: has_high}[dy]

    def when(cond, act):
        if cond is None:
            act()
        else:
            pl.when(cond)(act)

    count = [0]

    def fresh():
        count[0] += 1
        return count[0] - 1

    class Message:
        def __init__(self, src, dst, dx, dy):
            self.key, self.dy = fresh(), dy
            self.copy = lambda: pltpu.make_async_remote_copy(
                src_ref=src,
                dst_ref=dst,
                send_sem=sent.at[self.key],
                recv_sem=got.at[self.key],
                device_id=lateral(dx, dy),
                device_id_type=MESH,
            )

        def start(self):
            when(reaches(self.dy), lambda: self.copy().start())

        def receive(self):
            when(reaches(-self.dy), lambda: self.copy().wait_recv())

        def finish(self):
            when(reaches(self.dy), lambda: self.copy().wait_send())

    def vertical(src, dst, step):
        key = fresh()
        return pltpu.make_async_remote_copy(
            src_ref=src,
            dst_ref=dst,
            send_sem=sent.at[key],
            recv_sem=got.at[key],
            device_id={"frame": frame + step},
            device_id_type=MESH,
        )

    def local(src, dst):
        copies.append(pltpu.make_async_copy(src, dst, near_by.at[len(copies)]))
        return copies[-1]

    copies = []
    at = lambda i: pl.ds(i * BLOCK, BLOCK)
    part = lambda ref, start, size: ref.at[pl.ds(start, size)]
    pairs = lambda ref, side, start: ref.at[side, pl.ds(start, HALF)]
    mids = lambda i: key_ext.at[at(i), pl.ds(2 * RIM, rows - 2 * RIM)]
    both = lambda ref, start: ref.at[:, pl.ds(start, HALF)]

    feat_in = [local(feat_hbm.at[at(i)], feat_ref.at[at(i)]) for i in range(chunks)]
    cot_in = [local(cot_hbm.at[at(i)], cot_ref.at[at(i)]) for i in range(chunks)]

    down_edge = [
        vertical(both(own_edge, i * HALF), both(key_edge, (i + 1) * HALF), -1) for i in range(chunks)
    ]
    down_mid = [
        vertical(own_mid.at[at(i)], mids(i + 1), -1) for i in range(chunks)
    ]
    up_edge = [
        vertical(both(send_edge, i * HALF), both(recv_edge, i * HALF), 1) for i in range(chunks)
    ]
    up_mid = [vertical(send_mid.at[at(i)], recv_mid.at[at(i)], 1) for i in range(chunks)]
    key_lat = [
        [
            Message(pairs(key_edge, side, i * HALF), pairs(key_rim, 1 - side, i * HALF), 0, dy)
            for side, dy in ((0, -1), (1, 1))
        ]
        for i in range(chunks + 2)
    ]

    def key_side(dx):
        begin, end = (HALF, half + HALF) if dx < 0 else (half, 0)
        return [
            Message(mids(2 * begin // BLOCK), mids(2 * end // BLOCK), dx, 0),
            Message(both(key_edge, begin), both(key_edge, end), dx, 0),
        ]

    key_left, key_right = key_side(-1), key_side(1)
    back_lat = [
        [
            Message(pairs(send_rim, side, (i + 1) * HALF), pairs(recv_rim, 1 - side, i * HALF), 0, dy)
            for side, dy in ((0, -1), (1, 1))
        ]
        for i in range(chunks)
    ]

    def back_side(dx):
        side, begin = (0, 0) if dx < 0 else (1, half + HALF)
        return [
            Message(send_lon.at[side], recv_lon.at[side], dx, 0),
            Message(both(send_rim, begin), recv_corner.at[side], dx, 0),
        ]

    back_left, back_right = back_side(-1), back_side(1)

    barrier = pltpu.get_barrier_semaphore()

    def greet(device):
        pl.semaphore_signal(barrier, inc=1, device_id=device, device_id_type=MESH)

    pl.when(has_down)(lambda: greet({"frame": frame - 1}))
    pl.when(has_up)(lambda: greet({"frame": frame + 1}))
    one = lambda cond: jnp.where(cond, 1, 0)

    @pl.when(~has_up)
    def _():
        for copy in feat_in:
            copy.start()

    @pl.when(has_up)
    def _():
        for dx, dy in ((-1, 0), (1, 0), (0, -1), (0, 1)):
            when(reaches(dy), lambda: greet(lateral(dx, dy)))
        for copy in feat_in:
            copy.start()
        for copy in cot_in:
            copy.start()

    for copy in feat_in:
        copy.wait()

    @pl.when(has_down)
    def _():
        @pl.loop(0, half)
        def _(pos):
            first, second = feat_ref[2 * pos].astype(f32), feat_ref[2 * pos + 1].astype(f32)
            low = jnp.concatenate([first[:RIM], second[:RIM]], axis=0)
            high = jnp.concatenate([first[rows - RIM :], second[rows - RIM :]], axis=0)
            own_edge[0, pos] = low.astype(bf16)
            own_edge[1, pos] = high.astype(bf16)
            own_mid[2 * pos] = first[middle].astype(bf16)
            own_mid[2 * pos + 1] = second[middle].astype(bf16)

    lateral_count = 2 + one(has_low) + one(has_high)
    pl.semaphore_wait(barrier, one(has_down) + one(has_up) * (1 + lateral_count))

    @pl.when(has_down)
    def _():
        for i in (0, last, inner[0]):
            down_edge[i].start()
        down_mid[0].start()
        for i in inner[1:]:
            down_edge[i].start()
        for i in (last, *inner):
            down_mid[i].start()

    @pl.when(has_up)
    def _():
        for side, present in ((0, has_low), (1, has_high)):

            @pl.when(~present)
            def _():
                key_rim[side] = jnp.zeros(key_rim.shape[1:], bf16)
                recv_rim[side] = jnp.zeros(recv_rim.shape[1:], bf16)

        spread_ref[...] = spreader(wide)

        for begin in (0, cols + 2 * RIM - RAD):
            near_acc[pl.ds(begin, RAD)] = jnp.zeros((RAD, wide, chans), f32)

        def add(ref, start, value, held):
            if held:
                ref[pl.ds(start, held)] += value[:held]
            ref[pl.ds(start + held, value.shape[0] - held)] = value[held:]

        def back(i):
            cot_in[i].wait()
            cot = cot_ref[at(i)].reshape(BLOCK * rows, cot_ref.shape[2])
            spread = jnp.dot(cot, spread_ref[...], preferred_element_type=f32)
            split = band_near.shape[2]
            near = sheared(spread[:, :split], rows, [j * wide for j in range(BLOCK)])
            far = sheared(spread[:, split:], rows, [j // 2 * wide for j in range(BLOCK)])
            band_near[i] = near
            band_far[i] = far
            feats = feat_ref[at(i)].reshape(BLOCK * rows, chans)
            contract = (((0,), (0,)), ((), ()))
            grad = lax.dot_general(near, feats, contract, preferred_element_type=f32)
            grad = grad[: NEAR * wide].reshape(NEAR, wide, chans)
            add(near_acc, i * BLOCK + RAD, grad, i and NEAR - BLOCK)
            grad = lax.dot_general(far, feats, contract, preferred_element_type=f32)
            grad = grad[: FAR * wide].reshape(FAR, wide, chans)
            add(far_acc, i * (BLOCK // 2), grad, i and FAR - BLOCK // 2)

        def settle(pos):
            coarse = pair_sum(far_acc[pos]) * 0.25
            first = (near_acc[2 * pos] + coarse) * scale
            second = (near_acc[2 * pos + 1] + coarse) * scale
            for side, begin in ((0, 0), (1, RIM + rows)):
                cut = slice(begin, begin + RIM)
                send_rim[side, pos] = jnp.concatenate([first[cut], second[cut]], axis=0).astype(bf16)
            return first[RIM : RIM + rows], second[RIM : RIM + rows]

        def settle_side(side):
            @pl.loop(0, HALF, unroll=True)
            def _(pos):
                first, second = settle(pos + side * (half + HALF))
                send_lon[side, 2 * pos] = first.astype(bf16)
                send_lon[side, 2 * pos + 1] = second.astype(bf16)

            for message in (back_left, back_right)[side]:
                message.start()

        def settle_inner(i):
            @pl.loop(0, HALF, unroll=True)
            def _(pos):
                place = i * HALF + pos
                for k, value in enumerate(settle(place + HALF)):
                    near_acc[RIM + 2 * place + k, RIM : RIM + rows] = value
                    if 0 < i < last:
                        send_mid[2 * place + k] = value[middle].astype(bf16)

            if 0 < i < last:
                for message in back_lat[i]:
                    message.start()
                up_mid[i].start()

        def join_corner(i):
            side = int(i == 0)
            for message in (back_left, back_right)[side]:
                message.receive()

            @pl.loop(0, HALF, unroll=True)
            def _(pos):
                for k in range(2):
                    place = (i + 1) * HALF + pos
                    value = send_rim[k, place].astype(f32) + recv_corner[side, k, pos].astype(f32)
                    send_rim[k, place] = value.astype(bf16)

            for message in back_lat[i]:
                message.start()

        def forward_edge(i):
            down_edge[i].wait_recv()
            for message in key_lat[i + 1]:
                message.start()
            if i in (0, last):
                (key_left if i == 0 else key_right)[1].start()

        def forward_side(i):
            (key_right if i == 0 else key_left)[1].receive()
            for message in key_lat[0 if i == 0 else chunks + 1]:
                message.start()

        def forward_mid(i):
            down_mid[i].wait_recv()
            (key_left if i == 0 else key_right)[0].start()

        def rise_edge(i):
            for message in back_lat[i]:
                message.receive()

            @pl.loop(i * HALF, (i + 1) * HALF, unroll=True)
            def _(place):
                for side, begin in ((0, RIM), (1, rows)):
                    value = recv_rim[side, place].astype(f32)
                    own = [
                        near_acc[RIM + 2 * place + k, begin : begin + RIM] for k in range(2)
                    ]
                    value = value + jnp.concatenate(own, axis=0)
                    send_edge[side, place] = value.astype(bf16)

            up_edge[i].start()

        def rise_side(i):
            side = int(i == 0)

            @pl.loop(0, BLOCK)
            def _(pos):
                place = RIM + i * BLOCK + pos
                rim = recv_lon[side, pos].astype(f32)
                value = near_acc[place, RIM : RIM + rows] + rim
                near_acc[place, RIM : RIM + rows] = value
                send_mid[i * BLOCK + pos] = value[middle].astype(bf16)

            up_mid[i].start()

        for i in range(chunks):
            back(i)
            if i == 0:
                settle_side(0)
            elif i > 1:
                settle_inner(i - 1)
        settle_side(1)
        settle_inner(0)
        settle_inner(last)
        join_corner(last)
        forward_edge(0)
        forward_edge(last)
        rise_edge(inner[0])
        rise_edge(inner[1])
        forward_edge(inner[0])
        join_corner(0)
        rise_side(last)
        rise_edge(last)
        forward_side(0)
        forward_side(last)
        forward_mid(0)
        forward_edge(inner[1])
        rise_side(0)
        rise_edge(0)
        forward_mid(last)

        def unfold_edge(i):
            @pl.loop(i * HALF, (i + 1) * HALF, unroll=True)
            def _(pos):
                for side, begin in ((0, 0), (1, rows)):
                    pieces = [ref[side, pos].astype(f32) for ref in (key_rim, key_edge)[:: 1 - 2 * side]]
                    values = []
                    for k in range(2):
                        cut = slice(k * RIM, (k + 1) * RIM)
                        values.append(jnp.concatenate([piece[cut] for piece in pieces], axis=0))
                        key_ext[2 * pos + k, begin : begin + 2 * RIM] = values[k].astype(bf16)
                    pool[pos, begin : begin + 2 * RIM] = pooled(values)

        def unfold_mid(i):
            for pos in range(i * HALF, (i + 1) * HALF):
                values = [key_ext[2 * pos + k, 2 * RIM : rows].astype(f32) for k in range(2)]
                pool[pos, 2 * RIM : rows] = pooled(values)

        def pooled(values):
            return (pair_sum(values[0] + values[1]) * 0.25).astype(bf16)

        def own(i):
            keys = key_ext[pl.ds(i * BLOCK + RAD, NEAR)].reshape(NEAR * wide, chans)
            coarse = pool[pl.ds(i * (BLOCK // 2), FAR)].reshape(FAR * wide, chans)
            total = jnp.dot(band_near[i, :, : NEAR * wide], keys, preferred_element_type=f32)
            total += jnp.dot(band_far[i, :, : FAR * wide], coarse, preferred_element_type=f32)
            total = (total * scale).reshape(BLOCK, rows, chans)
            own_acc[at(i)] = total
            out_ref[at(i)] = total.astype(bf16)

        key_left[0].receive()
        key_right[0].receive()
        for i in (0, 1, chunks, chunks + 1):
            for message in key_lat[i]:
                message.receive()
        for i in (0, 1, last + 1, last + 2):
            unfold_edge(i)
            unfold_mid(i)
        for i in inner:
            for message in key_lat[i + 1]:
                message.receive()
            unfold_edge(i + 1)
            if i == inner[-1]:
                for group in key_lat + back_lat + [key_left, key_right, back_left, back_right]:
                    for message in group:
                        message.finish()

                @pl.when(has_down)
                def _():
                    for copy in down_edge + down_mid:
                        copy.wait_send()

            down_mid[i].wait_recv()
            unfold_mid(i + 1)
            own(i - 1)
        for i in range(inner[-1], chunks):
            own(i)

    for i in inner + [last, 0]:

        @pl.when(has_down)
        def _():
            up_mid[i].wait_recv()
            up_edge[i].wait_recv()

        def carried(place):
            edges = [recv_edge[side, place].astype(f32) for side in range(2)]
            for k in range(2):
                cut = slice(k * RIM, (k + 1) * RIM)
                mid = recv_mid[2 * place + k].astype(f32)
                yield 2 * place + k, jnp.concatenate([edges[0][cut], mid, edges[1][cut]], axis=0)

        @pl.when(has_down & has_up)
        def _():
            @pl.loop(i * HALF, (i + 1) * HALF, unroll=True)
            def _(place):
                for pos, value in carried(place):
                    out_ref[pos] = (own_acc[pos] + value).astype(bf16)

        @pl.when(has_down & ~has_up)
        def _():
            @pl.loop(i * HALF, (i + 1) * HALF, unroll=True)
            def _(place):
                for pos, value in carried(place):
                    out_ref[pos] = value.astype(bf16)

    @pl.when(has_down & ~has_up)
    def _():
        for copy in down_edge + down_mid:
            copy.wait_send()

    @pl.when(has_up)
    def _():
        for copy in up_edge + up_mid:
            copy.wait_send()


def body(sizes, features, cotangent):
    _, cols, rows, chans = features.shape
    wide = rows + 2 * RIM
    chunks, half = cols // BLOCK, cols // 2
    near, far = padded(NEAR * wide), padded(FAR * wide)
    vmem, hbm = (pl.BlockSpec(memory_space=space) for space in (pltpu.VMEM, pltpu.HBM))
    short = lambda *dims: pltpu.VMEM(dims + (chans,), jnp.bfloat16)
    full = lambda *dims: pltpu.VMEM(dims + (chans,), jnp.float32)
    messages = 8 * chunks + 12
    out = pl.pallas_call(
        functools.partial(kernel, sizes),
        out_shape=jax.ShapeDtypeStruct((cols, rows, chans), jnp.bfloat16),
        in_specs=[hbm] * 2,
        out_specs=vmem,
        scratch_shapes=[
            short(cols, rows),
            pltpu.VMEM((cols, rows, cotangent.shape[3]), jnp.bfloat16),
            pltpu.VMEM((cotangent.shape[3], near + far), jnp.bfloat16),
            short(2, half, 2 * RIM),
            short(cols, rows - 2 * RIM),
            short(2, half + RIM, 2 * RIM),
            short(2, half + RIM, 2 * RIM),
            short(cols + 2 * RIM, wide),
            short(half + RIM, wide),
            full(cols + 2 * RIM, wide),
            full(half + RIM, wide),
            pltpu.VMEM((chunks, BLOCK * rows, near), jnp.bfloat16),
            pltpu.VMEM((chunks, BLOCK * rows, far), jnp.bfloat16),
            short(2, RIM, rows),
            short(2, RIM, rows),
            short(2, half + RIM, 2 * RIM),
            short(2, half, 2 * RIM),
            short(2, 2, HALF, 2 * RIM),
            short(2, half, 2 * RIM),
            short(cols, rows - 2 * RIM),
            short(2, half, 2 * RIM),
            short(cols, rows - 2 * RIM),
            full(cols, rows),
            pltpu.SemaphoreType.DMA((2 * chunks,)),
            pltpu.SemaphoreType.DMA((messages,)),
            pltpu.SemaphoreType.DMA((messages,)),
        ],
        cost_estimate=pl.CostEstimate(flops=10**10, bytes_accessed=4 << 20, transcendentals=0),
        compiler_params=pltpu.CompilerParams(
            collective_id=0, has_side_effects=True, vmem_limit_bytes=54250 << 10
        ),
    )(features[0], cotangent[0])
    return out[None]


def solution(mesh):
    spec = P("frame", "lon", "lat", None)
    sizes = tuple(mesh.shape[axis] for axis in ("lon", "lat", "frame"))
    return jax.shard_map(
        functools.partial(body, sizes), mesh=mesh, in_specs=(spec, spec), out_specs=spec, check_vma=False
    )
```
